512 devices in a mesh: wide: 32 (over z, x), narrow: 16 (over y, core).
Axes of the slice: x: 4, y: 8, z: 8, core: 2. Of those that a mesh axis runs over, the one named last changes fastest.
Arguments:
- excitation: bfloat16 [64, 2097152], P(None, ('wide', 'narrow')), may hold values from -6 to 6
- coords: bfloat16 [3, 2097152], P(None, ('wide', 'narrow')), may hold values from 0 to 1
- basis: bfloat16 [16, 2097152], P(None, ('wide', 'narrow')), may hold values from -0.5 to 0.5
- couplings: bfloat16 [262144, 256], P(('wide', 'narrow')), may hold values from -1.5 to 1.5
- near_list: int32 [16384, 24], P(('wide', 'narrow')), may hold values from 0 to 95
- far_dest: int32 [262144, 1], P(('wide', 'narrow')), may hold values from 0 to 511; in each aligned block of 512 rows (0 to 511, 512 to 1023, ...) at most 2 rows name the same one
- far_slot: int32 [262144], P(('wide', 'narrow')), may hold values from 0 to 31
- far_src: int32 [262144], P(('wide', 'narrow')), may hold values from 0 to 31
Outputs:
- potentials: bfloat16 [64, 2097152], P(None, ('wide', 'narrow'))
The draws below stay inside these ranges and needn't reach their ends.
Inputs may be any that keep to these rules, and one draw needn't show every extreme that they name: `near_list`: k // 32 picks the previous (0), same (1) or next (2) device along narrow, k % 32 a cluster of it. `far_dest`: among the 512 pairs of one source device, at most 2 name the same receiving device; in some device's pairs one receiving device is named exactly 2 times.
All inputs are finite; a program needn't handle non-finite values.
Results may differ from the reference program's by a relative error of at most 0.0054.
Values may be sent and summed in bfloat16 or wider, within the bound.
A program may use at most 64 MiB of HBM per device.

```python
import math
import jax
import jax.numpy as jnp
import numpy as np
from jax import lax

PC = 128
R = 16
NRHS = 64
CL = 32
NEAR = 24
CLUSTERS = 16384
PANELS = 2097152
FARP = 512
CAP = 2
PAIRS = 262144
N_WIDE = 32
N_NARROW = 16
DEVICES = 512


def plant(array, own_key, least, largest):
    longest = array.shape.index(max(array.shape))
    spots = []
    for shift in (0, 1):
        where = [jax.random.randint(jax.random.fold_in(own_key, axis), (), 0, length) for axis, length in enumerate(array.shape)]
        where[longest] = (where[longest] + shift) % array.shape[longest]
        spots.append(tuple(where))
    return array.at[spots[0]].set(least).at[spots[1]].set(largest)


def shard_levels(own_key, dims, pieces, smallest, high):
    def one(axis_at, blocks):
        draws = jax.random.uniform(jax.random.fold_in(jax.random.fold_in(own_key, 6), axis_at), (blocks,), jnp.float32, smallest / len(pieces), high / len(pieces))
        return jnp.repeat(jnp.exp(draws), dims[axis_at] // blocks).reshape((-1,) + (1,) * (len(dims) - axis_at - 1))

    level = one(*pieces[0])
    for cut in pieces[1:]:
        level = level * one(*cut)
    return level


def assign_block(stream_key, own, number, rows, count, top, bound, slope):
    order = jax.random.permutation(stream_key, count)
    packed, usual = shares(count, rows * top, bound, slope, True), shares(count, rows * top, bound, slope, False)
    places = jnp.arange(count)

    def named(sizes, rotation):
        used = int((sizes > 0).sum())
        fixed = max(1, used // 4)
        shifted = fixed + (places - fixed + rotation * (used - fixed)) % max(1, count - fixed)
        return jnp.zeros((count,), jnp.int32).at[order[jnp.where(places < fixed, places, shifted)]].set(jnp.asarray(sizes, jnp.int32))

    sizes = jnp.where(number % 4 == 0, named(packed, number // 4), named(usual, number - number // 4 - 1))
    mixed = jax.random.permutation(jax.random.fold_in(own, 3), count)
    giver, sink = mixed[0:count // 2 * 2:2], mixed[1:count // 2 * 2:2]
    room = jnp.minimum(sizes[giver] - 1, bound - sizes[sink]) // 2
    room = jnp.where((giver == order[0]) | (sink == order[0]) | (sizes[sink] == 0), 0, jnp.maximum(room, 0))
    shifted = jax.random.randint(jax.random.fold_in(own, 4), (count // 2,), 0, 1 << 20) % (room + 1)
    sizes = sizes.at[giver].add(-shifted).at[sink].add(shifted)
    items = jnp.searchsorted(jnp.cumsum(sizes), jnp.arange(rows * top), side="right").astype(jnp.int32)
    table = items.reshape(top, rows).T
    table = table[jax.random.permutation(jax.random.fold_in(own, 1), rows)]
    rotation = jax.random.randint(jax.random.fold_in(own, 2), (rows, 1), 0, top)
    return jnp.take_along_axis(table, (jnp.arange(top)[None, :] + rotation) % top, axis=1)


def shares(amount, total, most, skew, full):
    portions = [(1 << 20) // math.isqrt(standing ** skew) + 1 for standing in range(1, amount + 1)]
    largest = most if full else min(most, max(-(-total // amount), total * portions[0] // sum(portions)))
    least = 1 if total - largest >= amount - 1 else 0
    given, rest = [largest] + [least] * (amount - 1), total - largest - least * (amount - 1)
    while rest > 0:
        candidates = [i for i in range(1, amount) if given[i] < largest] or [i for i in range(1, amount) if given[i] < most]
        mass, left = sum([portions[i] for i in candidates]), rest
        for i in candidates:
            addition = min(most - given[i], max(1, left * portions[i] // mass), rest)
            given[i] = given[i] + addition
            rest = rest - addition
    return np.array(given)


def centred(key, dims, width, limit, cuts=(), held_as=jnp.bfloat16):
    array = jax.random.normal(key, dims, jnp.float32) * width
    if len(cuts) > 0:
        array = shard_levels(key, dims, cuts, -0.22, 0.18) * array
    return jnp.clip(array, min=-limit, max=limit).astype(held_as)


def setup_inputs(seed: int = 0) -> dict:
    keys = jax.random.split(jax.random.key(seed), 9)
    excitation = centred(keys[0], (NRHS, PANELS), 1.0, 6.0, ((1, 512),))
    coords = jnp.clip(1.0 * jax.random.uniform(keys[1], (3, PANELS), jnp.float32) ** shard_levels(keys[1], (3, PANELS), ((1, 512),), -0.2, 0.2), 0.0, 1.0).astype(jnp.bfloat16)
    basis = centred(keys[2], (R, PANELS), PC ** -0.5, 0.5, ((1, 512),))
    couplings = centred(keys[3], (PAIRS, R * R), R ** -0.5, 1.5, ((0, 512),))
    near_list = plant(jax.random.randint(keys[4], (CLUSTERS, NEAR), 0, 3 * CL), jax.random.fold_in(keys[4], 1), 0, (3 * CL) - 1).astype(jnp.int32)
    far_dest_keys = jax.random.split(jax.random.fold_in(keys[5], 1), PAIRS // FARP)
    far_dest_turns = jax.random.permutation(jax.random.fold_in(keys[5], 3), PAIRS // FARP)
    far_dest = jax.vmap(lambda own, number: assign_block(jax.random.fold_in(keys[5], 2), own, number, FARP, DEVICES, 1, CAP, 1))(far_dest_keys, far_dest_turns).reshape((PAIRS, 1))
    far_slot = plant(jax.random.randint(keys[6], (PAIRS,), 0, CL), jax.random.fold_in(keys[6], 1), 0, CL - 1).astype(jnp.int32)
    far_src = plant(jax.random.randint(keys[7], (PAIRS,), 0, CL), jax.random.fold_in(keys[7], 1), 0, CL - 1).astype(jnp.int32)
    return dict(excitation=excitation, coords=coords, basis=basis, couplings=couplings, near_list=near_list, far_dest=far_dest, far_slot=far_slot, far_src=far_src)


SOFTEN = 0.0025

def near_field(field_window, coord_window, coord_own, lists):
    columns_count = field_window.shape[0]
    clusters = lists.shape[0]
    panels = coord_own.shape[1] // clusters
    kernel_scale = 1.0 / math.sqrt(panels * lists.shape[1])
    field_blocks = field_window.reshape(columns_count, 3 * clusters, panels)
    coord_blocks = coord_window.reshape(3, 3 * clusters, panels).astype(jnp.float32)
    target = coord_own.reshape(3, clusters, panels).astype(jnp.float32)

    def one_entry(running, column):
        source_field = jnp.take(field_blocks, column, axis=1)
        source_coord = jnp.take(coord_blocks, column, axis=1)
        distance = jnp.full((clusters, panels, panels), SOFTEN, jnp.float32)
        for axis_id in range(3):
            spacing = target[axis_id][:, :, None] - source_coord[axis_id][:, None, :]
            distance = distance + spacing * spacing
        kernel = (kernel_scale * lax.rsqrt(distance)).astype(jnp.bfloat16)
        running = running + jnp.einsum('cts,ncs->nct', kernel.astype(jnp.float32), source_field.astype(jnp.float32))
        return (running, None)
    initial = jnp.zeros((columns_count, clusters, panels), jnp.float32)
    running, _ = lax.scan(one_entry, initial, lists.T)
    return running.reshape(columns_count, clusters * panels)

def reference(excitation, coords, basis, couplings, near_list, far_dest, far_slot, far_src):
    own_panels = CL * PC
    basis_blocks = basis.reshape(R, CLUSTERS, PC).astype(jnp.float32)
    coefficients = jnp.einsum('ncp,rcp->cnr', excitation.reshape(NRHS, CLUSTERS, PC).astype(jnp.float32), basis_blocks).astype(jnp.bfloat16)

    def far_step(carry, items):
        device, blocks, dest, slot, source = items
        chosen = jnp.take(coefficients, device * CL + source, axis=0)
        records = jnp.einsum('pab,pnb->pna', blocks.reshape(FARP, R, R).astype(jnp.float32), chosen.astype(jnp.float32)).astype(jnp.bfloat16)
        records = lax.optimization_barrier(records).astype(jnp.float32)
        carry = carry.at[dest * CL + slot].add(records)
        return (carry, None)
    far_sums, _ = lax.scan(far_step, jnp.zeros((CLUSTERS, NRHS, R), jnp.float32), (jnp.arange(DEVICES, dtype=jnp.int32), couplings.reshape(DEVICES, FARP, R * R), far_dest.reshape(DEVICES, FARP), far_slot.reshape(DEVICES, FARP), far_src.reshape(DEVICES, FARP)))
    far_rounded = far_sums.astype(jnp.bfloat16)
    far_field = jnp.einsum('cnr,rcp->ncp', far_rounded.astype(jnp.float32), basis_blocks).reshape(NRHS, PANELS)
    field_grid = jnp.pad(excitation.reshape(NRHS, N_WIDE, N_NARROW, own_panels).transpose(1, 2, 0, 3), ((0, 0), (1, 1), (0, 0), (0, 0)))
    coord_grid = jnp.pad(coords.reshape(3, N_WIDE, N_NARROW, own_panels).transpose(1, 2, 0, 3), ((0, 0), (1, 1), (0, 0), (0, 0)))
    own_coords = coords.reshape(3, DEVICES, own_panels).transpose(1, 0, 2)
    lists_all = near_list.reshape(DEVICES, CL, NEAR)

    def per_device(device):
        wide_index = (device // N_NARROW).astype(jnp.int32)
        narrow_index = (device % N_NARROW).astype(jnp.int32)
        anchor = jnp.zeros((), jnp.int32)
        field_window = lax.dynamic_slice(field_grid, (wide_index, narrow_index, anchor, anchor), (1, 3, NRHS, own_panels))[0]
        field_window = field_window.transpose(1, 0, 2).reshape(NRHS, 3 * own_panels)
        coord_window = lax.dynamic_slice(coord_grid, (wide_index, narrow_index, anchor, anchor), (1, 3, 3, own_panels))[0]
        coord_window = coord_window.transpose(1, 0, 2).reshape(3, 3 * own_panels)
        own = lax.dynamic_index_in_dim(own_coords, device, 0, keepdims=False)
        lists = lax.dynamic_index_in_dim(lists_all, device, 0, keepdims=False)
        return near_field(field_window, coord_window, own, lists)
    near = lax.map(per_device, jnp.arange(DEVICES, dtype=jnp.int32))
    near = near.transpose(1, 0, 2).reshape(NRHS, PANELS)
    return (near + far_field).astype(jnp.bfloat16)
```

```python
import functools
import math

import jax
import jax.numpy as jnp
from jax import lax
from jax.experimental import pallas as pl
from jax.experimental.pallas import tpu as pltpu
from jax.sharding import PartitionSpec as P

SOFTEN = 0.0025


def neighbours(value):
    devices = lax.axis_size("narrow")
    up = [(i, (i + 1) % devices) for i in range(devices - 1)]
    down = [(j, i) for i, j in up]
    return (lax.ppermute(value, "narrow", up), value, lax.ppermute(value, "narrow", down))


def split(value):
    high = value.astype(jnp.bfloat16).astype(jnp.float32)
    rest = value - high
    middle = rest.astype(jnp.bfloat16).astype(jnp.float32)
    return (high, middle, rest - middle)


def near_kernel(
    clusters, entries, panels, lists, field_before, field_own, field_after, coord_before, coord_own, coord_after,
    out, field, raw, sources, targets, sems,
):
    own = clusters * panels
    group = panels // 16
    copies = [
        pltpu.make_async_copy(part, field.at[:, pl.ds(i * own, own)], sems.at[i])
        for i, part in enumerate((field_before, field_own, field_after))
    ]
    for copy in copies:
        copy.start()
    raw[...] = jnp.zeros_like(raw)
    ones = jnp.ones((3, own), jnp.float32)
    lane_group = lax.broadcasted_iota(jnp.int32, (panels, panels), 1) // 16
    for i, part in enumerate((coord_before, coord_own, coord_after)):
        where = part[...].astype(jnp.float32)
        square = where[0:1] * where[0:1] + where[1:2] * where[1:2] + where[2:3] * where[2:3]
        if i == 1:
            raw[0:3, :] = where
            raw[6:9, :] = ones
            for row, value in enumerate(split(square + SOFTEN)):
                raw[3 + row : 4 + row, :] = value
            rows = raw[...].astype(jnp.bfloat16)
            for r in range(group):
                targets[16 * r : 16 * r + 16, :] = rows
        raw[0:3, :] = -2.0 * where
        raw[3:6, :] = ones
        for row, value in enumerate(split(square)):
            raw[6 + row : 7 + row, :] = value
        for g in range(clusters // group):
            block = jnp.concatenate(
                [raw[:, (group * g + r) * panels : (group * g + r + 1) * panels] for r in range(group)], axis=0
            ).T
            for r in range(group):
                start = (i * clusters + group * g + r) * panels
                sources[start : start + panels, :] = jnp.where(lane_group == r, block, 0.0).astype(jnp.bfloat16)
    for copy in copies:
        copy.wait()
    scale = 1.0 / math.sqrt(panels * entries)

    @pl.loop(0, clusters)
    def _(cluster):
        columns = pl.ds(pl.multiple_of(cluster * panels, panels), panels)
        target = targets[:, columns]
        total = jnp.zeros((out.shape[0], panels), jnp.float32)
        for entry in range(entries):
            source = pl.ds(pl.multiple_of(lists[cluster * entries + entry] * panels, panels), panels)
            distance = jnp.dot(sources[source, :], target, preferred_element_type=jnp.float32)
            kernel = lax.rsqrt(distance).astype(jnp.bfloat16)
            total += jnp.dot(field[:, source], kernel, preferred_element_type=jnp.float32)
        out[:, columns] = total * scale


def near_field(fields, coords, lists):
    clusters, entries = lists.shape
    columns_count, own = fields[1].shape
    panels = own // clusters
    whole = pl.BlockSpec(memory_space=pltpu.VMEM)
    anywhere = pl.BlockSpec(memory_space=pl.ANY)
    return pl.pallas_call(
        functools.partial(near_kernel, clusters, entries, panels),
        out_shape=jax.ShapeDtypeStruct((columns_count, own), jnp.float32),
        in_specs=[pl.BlockSpec(memory_space=pltpu.SMEM)] + [anywhere] * 3 + [whole] * 3,
        out_specs=whole,
        scratch_shapes=[
            pltpu.VMEM((columns_count, 3 * own), jnp.bfloat16),
            pltpu.VMEM((16, own), jnp.float32),
            pltpu.VMEM((3 * own, panels), jnp.bfloat16),
            pltpu.VMEM((panels, own), jnp.bfloat16),
            pltpu.SemaphoreType.DMA((3,)),
        ],
        compiler_params=pltpu.CompilerParams(vmem_limit_bytes=32 << 20),
        cost_estimate=pl.CostEstimate(flops=40_000_000_000, bytes_accessed=3_000_000, transcendentals=12_000_000),
    )(lists.reshape(-1), *fields, *coords)


def shards(excitation, coords, basis, couplings, near_list, far_dest, far_slot, far_src):
    columns_count, own_panels = excitation.shape
    clusters = near_list.shape[0]
    panels = own_panels // clusters
    basis_rank = basis.shape[0]
    pairs = far_src.shape[0]
    wide_count = lax.axis_size("wide")
    narrow_count = lax.axis_size("narrow")
    devices = wide_count * narrow_count
    capacity = max(2, 2 * pairs // devices)
    features = columns_count * basis_rank
    basis_blocks = basis.reshape(basis_rank, clusters, panels)
    coefficients = jnp.einsum(
        "ncp,rcp->cnr",
        excitation.reshape(columns_count, clusters, panels),
        basis_blocks,
        preferred_element_type=jnp.float32,
    ).astype(jnp.bfloat16)
    chosen = jnp.take(coefficients, far_src, axis=0)
    records = jnp.einsum(
        "pab,pnb->pna",
        couplings.reshape(pairs, basis_rank, basis_rank),
        chosen,
        preferred_element_type=jnp.float32,
    ).astype(jnp.bfloat16)
    records = records.reshape(pairs, features)
    destination = far_dest[:, 0]
    same_dest = destination[:, None] == destination[None, :]
    earlier = lax.broadcasted_iota(jnp.int32, (pairs, pairs), 1) < lax.broadcasted_iota(
        jnp.int32, (pairs, pairs), 0
    )
    order_within = jnp.sum((same_dest & earlier).astype(jnp.int32), axis=1)
    position = destination * capacity + order_within
    outgoing = jnp.zeros((devices * capacity, features), jnp.bfloat16).at[position].set(records)
    labels = jnp.full((devices * capacity,), -1, jnp.int32).at[position].set(far_slot)
    outgoing = outgoing.reshape(wide_count, narrow_count, capacity, features)
    labels = labels.reshape(wide_count, narrow_count, capacity)
    incoming, arrived = (
        lax.all_to_all(
            lax.all_to_all(outgoing, "wide", split_axis=0, concat_axis=0, tiled=True),
            "narrow",
            split_axis=1,
            concat_axis=1,
            tiled=True,
        ),
        lax.all_to_all(
            lax.all_to_all(labels, "wide", split_axis=0, concat_axis=0, tiled=True),
            "narrow",
            split_axis=1,
            concat_axis=1,
            tiled=True,
        ),
    )
    incoming = incoming.reshape(devices * capacity, features)
    arrived = arrived.reshape(devices * capacity)
    selector = (
        arrived[None, :] == lax.broadcasted_iota(jnp.int32, (clusters, devices * capacity), 0)
    ).astype(jnp.bfloat16)
    far_sums = jnp.dot(selector, incoming, preferred_element_type=jnp.float32)
    far_rounded = far_sums.astype(jnp.bfloat16).reshape(clusters, columns_count, basis_rank)
    far_field = jnp.einsum(
        "cnr,rcp->ncp", far_rounded, basis_blocks, preferred_element_type=jnp.float32
    ).reshape(columns_count, own_panels)
    near = near_field(neighbours(excitation), neighbours(coords), near_list)
    return (near + far_field).astype(jnp.bfloat16)


def solution(mesh):
    placed = (
        P(None, ("wide", "narrow")),
        P(None, ("wide", "narrow")),
        P(None, ("wide", "narrow")),
        P(("wide", "narrow"), None),
        P(("wide", "narrow"), None),
        P(("wide", "narrow"), None),
        P(("wide", "narrow")),
        P(("wide", "narrow")),
    )
    return jax.shard_map(
        shards, mesh=mesh, in_specs=placed, out_specs=P(None, ("wide", "narrow")), check_vma=False
    )
```

```python
import functools
import math

import jax
import jax.numpy as jnp
from jax import lax
from jax.experimental import pallas as pl
from jax.experimental.pallas import tpu as pltpu
from jax.sharding import PartitionSpec as P

SOFTEN = 0.0025
EARLY = 24
BF = jnp.bfloat16
F32 = jnp.float32
MESH = pl.DeviceIdType.MESH
NT = (((1,), (1,)), ((), ()))
WHOLE = pl.BlockSpec(memory_space=pltpu.VMEM)
ANYWHERE = pl.BlockSpec(memory_space=pl.ANY)


def onehot(condition):
    return jnp.where(condition, 1.0, 0.0).astype(BF)


def iota(shape, axis):
    return lax.broadcasted_iota(jnp.int32, shape, axis)


def split(value):
    high = value.astype(BF).astype(F32)
    rest = value - high
    middle = rest.astype(BF).astype(F32)
    return (high, middle, rest - middle)


def placement(sizes, dest, order):
    wide, narrow = sizes
    last = narrow // 2
    first = dest // (narrow * wide // last)
    across = (dest % narrow) // 2
    half_a = (dest % (narrow * wide // last), first * 2 + order, first)
    half_b = ((dest // narrow) * 2 + dest % 2, across * 2 + order, across)
    return (half_a, half_b)


def records_kernel(
    sizes, clusters, excitation, basis, couplings, dest, slot, source,
    send_a, send_b, label_a, label_b, blocks,
    coefficients, records,
):
    pairs, squared = couplings.shape
    rank = basis.shape[0]
    columns = excitation.shape[0]
    panels = excitation.shape[1] // clusters
    group = panels // rank
    for c in range(clusters):
        cut = slice(c * panels, (c + 1) * panels)
        blocks[c] = excitation[:, cut]
        coefficients[c * rank : (c + 1) * rank, :] = lax.dot_general(
            basis[:, cut], excitation[:, cut], NT, preferred_element_type=F32
        ).astype(BF)
    dest_down = jnp.broadcast_to(dest[...], (pairs, pairs))
    dest_along = jnp.broadcast_to(dest[...].astype(F32), (pairs, 128)).T[0:1].astype(jnp.int32)
    source_down = jnp.broadcast_to(source[...].astype(F32), (128, pairs)).T.astype(jnp.int32)
    same = (dest_down == dest_along) & (iota((pairs, pairs), 0) < iota((pairs, pairs), 1))
    order = jnp.sum(jnp.where(same, 1.0, 0.0), axis=0, keepdims=True).astype(jnp.int32)
    block = 128
    width = clusters * rank

    @pl.loop(0, rank // 2)
    def _(pair):
        lane = iota((squared, width), 1) % rank
        row = iota((squared, width), 0)
        spread = [onehot(row == (2 * pair + i) * rank + lane) for i in range(2)]
        for q in range(0, pairs, block):
            mine = jnp.concatenate([source_down[q : q + block]] * (width // 128), 1) == iota((block, width), 1) // rank
            parts = []
            for i in range(2):
                tiled = jnp.dot(couplings[q : q + block, :], spread[i], preferred_element_type=F32)
                chosen = jnp.where(mine, tiled, 0.0).astype(BF)
                parts.append(jnp.dot(chosen, coefficients[...], preferred_element_type=F32))
            records[q : q + block, pl.ds(pl.multiple_of(pair * 128, 128), 128)] = jnp.concatenate(parts, 1).astype(BF)

    half = records.shape[1] // 2
    for at, (partner, row, part), send, label in zip(
        (0, half), placement(sizes, dest_along, order), (send_a, send_b), (label_a, label_b)
    ):
        partners, rows = send.shape[0], send.shape[1]
        position = partner * rows + row
        for p in range(0, partners, 16):
            choice = onehot(position == iota((16 * rows, pairs), 0) + p * rows)
            packed = jnp.dot(choice, records[:, at : at + half], preferred_element_type=F32).astype(BF)
            send[p : p + 16] = packed.reshape(16, rows, half)
        code = (slot[...] + clusters * part + 1).astype(F32)
        left = jnp.where(partner == iota((partners, pairs), 0), code, 0.0).astype(BF)
        codes = lax.dot_general(left, onehot(row == iota((128, pairs), 0)), NT, preferred_element_type=F32)
        for p in range(partners):
            label[p] = codes[p : p + 1]


def outgoing(sizes, excitation, basis, couplings, far_dest, far_slot, far_src, clusters):
    columns, rank = excitation.shape[0], basis.shape[0]
    pairs = couplings.shape[0]
    wide, narrow = sizes
    last = narrow // 2
    partners = wide * narrow // last
    half = columns * rank // 2
    message = jax.ShapeDtypeStruct((partners, 2 * last, half), BF)
    codes = jax.ShapeDtypeStruct((partners, 1, 128), F32)
    blocks = jax.ShapeDtypeStruct((clusters, columns, excitation.shape[1] // clusters), BF)
    return pl.pallas_call(
        functools.partial(records_kernel, sizes, clusters),
        out_shape=(message, message, codes, codes, blocks),
        in_specs=[WHOLE] * 6,
        out_specs=(WHOLE,) * 5,
        scratch_shapes=[pltpu.VMEM((clusters * rank, columns), BF), pltpu.VMEM((pairs, 2 * half), BF)],
        compiler_params=pltpu.CompilerParams(vmem_limit_bytes=32 << 20),
    )(excitation, basis, couplings, far_dest, far_slot.reshape(1, pairs), far_src.reshape(1, pairs))


def main_kernel(
    sizes, clusters, entries, early,
    lists, coords, basis, send_a, send_b, label_a, label_b, excitation,
    out, field, coord_before, coord_after, raw, sources, targets, near,
    got_a, got_b, code_a, code_b, codes, part_a, part_b, sum_a, sum_b, spread,
    local_sem, halo_send, halo_recv, first_send, first_recv, last_send, last_recv,
):
    wide, narrow = sizes
    last = narrow // 2
    short = wide // last
    w, n = lax.axis_index("wide"), lax.axis_index("narrow")
    z, x, y, core = w // short, w % short, n // 2, n % 2
    columns, panels = excitation.shape[1:]
    own = clusters * panels
    rank = basis.shape[0]
    after, before = (n + 1) % narrow, (n + narrow - 1) % narrow

    halo = []
    for i, (source, target, device) in enumerate((
        (excitation, field.at[pl.ds(0, clusters)], after),
        (excitation, field.at[pl.ds(2 * clusters, clusters)], before),
        (coords, coord_before, after),
        (coords, coord_after, before),
    )):
        copy = pltpu.make_async_remote_copy(
            src_ref=source, dst_ref=target, send_sem=halo_send.at[i], recv_sem=halo_recv.at[i],
            device_id=(w, device), device_id_type=MESH,
        )
        copy.start()
        halo.append(copy)
    mine = pltpu.make_async_copy(excitation, field.at[pl.ds(clusters, clusters)], local_sem.at[0])
    mine.start()

    partners = send_a.shape[0]
    me_a, me_b = x * narrow + n, w * 2 + core

    def device_a(p):
        return (z * short + p // narrow, p % narrow)

    def device_b(p):
        return (p // 2, y * 2 + p % 2)

    groups = ((me_a, device_a, ((label_a, code_a), (send_a, got_a))), (me_b, device_b, ((label_b, code_b), (send_b, got_b))))

    @pl.loop(1, partners)
    def _(step):
        for g, (me, device, streams) in enumerate(groups):
            partner = (me + step) % partners
            for i, (send, got) in enumerate(streams):
                pltpu.make_async_remote_copy(
                    src_ref=send.at[partner], dst_ref=got.at[me],
                    send_sem=first_send.at[2 * g + i], recv_sem=first_recv.at[2 * g + i],
                    device_id=device(partner), device_id_type=MESH,
                ).start()

    for g, (me, device, streams) in enumerate(groups):
        for i, (send, got) in enumerate(streams):
            pltpu.make_async_copy(send.at[me], got.at[me], first_recv.at[2 * g + i]).start()

    group = panels // 16
    raw[...] = jnp.zeros_like(raw)
    ones = jnp.ones((3, own), F32)
    lane_group = iota((panels, panels), 1) // 16

    def prepare(i, part):
        where = part[...].astype(F32)
        square = where[0:1] * where[0:1] + where[1:2] * where[1:2] + where[2:3] * where[2:3]
        if i == 1:
            raw[0:3, :] = where
            raw[6:9, :] = ones
            for row, value in enumerate(split(square + SOFTEN)):
                raw[3 + row : 4 + row, :] = value
            rows = raw[...].astype(BF)
            for r in range(group):
                targets[16 * r : 16 * r + 16, :] = rows
        raw[0:3, :] = -2.0 * where
        raw[3:6, :] = ones
        for row, value in enumerate(split(square)):
            raw[6 + row : 7 + row, :] = value
        for g in range(clusters // group):
            block = jnp.concatenate(
                [raw[:, (group * g + r) * panels : (group * g + r + 1) * panels] for r in range(group)], axis=0
            ).T
            for r in range(group):
                sources[i * clusters + group * g + r] = jnp.where(lane_group == r, block, 0.0).astype(BF)

    prepare(1, coords)
    mine.wait()
    for copy in halo:
        copy.wait()
    prepare(0, coord_before)
    prepare(2, coord_after)

    @pl.when(n == 0)
    def _():
        field[0:clusters] = jnp.zeros((clusters, columns, panels), BF)

    @pl.when(n == narrow - 1)
    def _():
        field[2 * clusters : 3 * clusters] = jnp.zeros((clusters, columns, panels), BF)

    scale = 1.0 / math.sqrt(panels * entries)

    def near_clusters(start, stop):
        @pl.loop(start, stop)
        def _(cluster):
            cut = pl.ds(pl.multiple_of(cluster * panels, panels), panels)
            target = targets[:, cut]
            total = jnp.zeros((columns, panels), F32)
            for entry in range(entries):
                source = lists[cluster * entries + entry]
                distance = jnp.dot(sources[source], target, preferred_element_type=F32)
                kernel = lax.rsqrt(distance).astype(BF)
                total += jnp.dot(field[source], kernel, preferred_element_type=F32)
            near[:, cut] = total * scale

    near_clusters(0, early)

    rows = send_a.shape[1]
    half = send_a.shape[2]
    lasts = []
    for g, (got, code, part, final) in enumerate(((got_a, code_a, part_a, sum_a), (got_b, code_b, part_b, sum_b))):
        pltpu.make_async_copy(code, code, first_recv.at[2 * g]).wait()
        pltpu.make_async_copy(got, got, first_recv.at[2 * g + 1]).wait()
        for p in range(partners):
            codes[p : p + 1, :] = code[p]
        slots = partners * rows
        copied = jnp.dot(
            onehot(iota((slots, partners), 0) // rows == iota((slots, partners), 1)),
            codes[...].astype(BF),
            preferred_element_type=F32,
        )
        picked = jnp.where(iota((slots, 128), 0) % rows == iota((slots, 128), 1), copied, 0.0).astype(BF)
        along = lax.dot_general(jnp.ones((8, 128), BF), picked, NT, preferred_element_type=F32)[0:1].astype(jnp.int32)
        arrived = got[...].reshape(slots, half)
        for p in range(0, last, 2):
            choice = onehot(along == iota((2 * clusters, slots), 0) + (p * clusters + 1))
            sums = jnp.dot(choice, arrived, preferred_element_type=F32).astype(BF)
            part[p : p + 2] = sums.reshape(2, clusters, half)
        me = z if g == 0 else y

        @pl.loop(1, last)
        def _(step):
            there = (me + step) % last
            device = (there * short + x, n) if g == 0 else (w, there * 2 + core)
            pltpu.make_async_remote_copy(
                src_ref=part.at[there], dst_ref=final.at[me], send_sem=last_send.at[g], recv_sem=last_recv.at[g],
                device_id=device, device_id_type=MESH,
            ).start()

        pltpu.make_async_copy(part.at[me], final.at[me], last_recv.at[g]).start()

    near_clusters(early, clusters)

    count = rank // 2
    for g, final in enumerate((sum_a, sum_b)):
        pltpu.make_async_copy(final, final, last_recv.at[g]).wait()
        total = final[0].astype(F32)
        for p in range(1, last):
            total += final[p].astype(F32)
        total = total.astype(BF).astype(F32)
        for a in range(count):
            at = (g * count + a) * clusters
            spread[at : at + clusters, :] = total[:, a * columns : (a + 1) * columns]
    for c in range(clusters):
        cut = slice(c * panels, (c + 1) * panels)
        weights = spread[pl.ds(c, rank, stride=clusters), :].T.astype(BF)
        far = jnp.dot(weights, basis[:, cut], preferred_element_type=F32)
        out[:, cut] = (near[:, cut] + far).astype(BF)

    for g, (me, device, streams) in enumerate(groups):
        for i, (send, got) in enumerate(streams):
            most = pl.ds(0, partners - 1)
            pltpu.make_async_copy(send.at[most], send.at[most], first_send.at[2 * g + i]).wait()
    for g, part in enumerate((part_a, part_b)):
        most = pl.ds(0, last - 1)
        pltpu.make_async_copy(part.at[most], part.at[most], last_send.at[g]).wait()


def shards(excitation, coords, basis, couplings, near_list, far_dest, far_slot, far_src):
    columns, own = excitation.shape
    clusters, entries = near_list.shape
    panels = own // clusters
    rank = basis.shape[0]
    sizes = (lax.axis_size("wide"), lax.axis_size("narrow"))
    sent = outgoing(sizes, excitation, basis, couplings, far_dest, far_slot, far_src, clusters)
    partners, rows, half = sent[0].shape
    last = rows // 2
    dma = pltpu.SemaphoreType.DMA
    return pl.pallas_call(
        functools.partial(main_kernel, sizes, clusters, entries, EARLY),
        out_shape=jax.ShapeDtypeStruct((columns, own), BF),
        in_specs=[pl.BlockSpec(memory_space=pltpu.SMEM), WHOLE, WHOLE] + [ANYWHERE] * 5,
        out_specs=WHOLE,
        scratch_shapes=[
            pltpu.VMEM((3 * clusters, columns, panels), BF),
            pltpu.VMEM(coords.shape, BF),
            pltpu.VMEM(coords.shape, BF),
            pltpu.VMEM((16, own), F32),
            pltpu.VMEM((3 * clusters, panels, panels), BF),
            pltpu.VMEM((panels, own), BF),
            pltpu.VMEM((columns, own), F32),
        ]
        + [pltpu.VMEM((partners, rows, half), BF)] * 2
        + [pltpu.VMEM((partners, 1, 128), F32)] * 2
        + [pltpu.VMEM((partners, 128), F32)]
        + [pltpu.VMEM((last, clusters, half), BF)] * 4
        + [pltpu.VMEM((rank * clusters, columns), F32)]
        + [dma((1,)), dma((4,)), dma((4,)), dma((4,)), dma((4,)), dma((2,)), dma((2,))],
        compiler_params=pltpu.CompilerParams(vmem_limit_bytes=40 << 20, has_side_effects=True),
        cost_estimate=pl.CostEstimate(flops=40_000_000_000, bytes_accessed=6_000_000, transcendentals=12_000_000),
    )(near_list.reshape(-1), coords, basis, *sent)


def solution(mesh):
    placed = (
        P(None, ("wide", "narrow")),
        P(None, ("wide", "narrow")),
        P(None, ("wide", "narrow")),
        P(("wide", "narrow"), None),
        P(("wide", "narrow"), None),
        P(("wide", "narrow"), None),
        P(("wide", "narrow")),
        P(("wide", "narrow")),
    )
    return jax.shard_map(
        shards, mesh=mesh, in_specs=placed, out_specs=P(None, ("wide", "narrow")), check_vma=False
    )
```

```python
import functools
import math

import jax
import jax.numpy as jnp
from jax import lax
from jax.experimental import pallas as pl
from jax.experimental.pallas import tpu as pltpu
from jax.sharding import PartitionSpec as P

SOFTEN = 0.0025
FIRST_NEAR = 20
SECOND_NEAR = 25
BF = jnp.bfloat16
F32 = jnp.float32
MESH = pl.DeviceIdType.MESH
NT = (((1,), (1,)), ((), ()))
WHOLE = pl.BlockSpec(memory_space=pltpu.VMEM)
ANYWHERE = pl.BlockSpec(memory_space=pltpu.HBM)


def onehot(condition):
    return jnp.where(condition, 1.0, 0.0).astype(BF)


def iota(shape, axis):
    return lax.broadcasted_iota(jnp.int32, shape, axis)


def split(value):
    high = value.astype(BF).astype(F32)
    rest = value - high
    middle = rest.astype(BF).astype(F32)
    return (high, middle, rest - middle)


def placement(sizes, dest, order):
    wide, narrow = sizes
    last = narrow // 2
    first = dest // (narrow * wide // last)
    across = (dest % narrow) // 2
    half_a = (dest % (narrow * wide // last), first * 2 + order, first)
    half_b = ((dest // narrow) * 2 + dest % 2, across * 2 + order, across)
    return (half_a, half_b)


def main_kernel(
    sizes, clusters, entries,
    lists, excitation, coords, basis, couplings, dest, slot, origin,
    out, field, coord_before, coord_after, raw, sources, targets, near,
    own_field, own_coords, own_basis, own_couplings, source_down, coefficients, records,
    send_a, send_b, label_a, label_b,
    got_a, got_b, code_a, code_b, codes, part_a, part_b, sum_a, sum_b, spread,
    local_sem, halo_send, halo_recv, first_send, first_recv, last_send, last_recv,
):
    wide, narrow = sizes
    last = narrow // 2
    short = wide // last
    w, n = lax.axis_index("wide"), lax.axis_index("narrow")
    z, x, y, core = w // short, w % short, n // 2, n % 2
    columns, own = excitation.shape
    panels = own // clusters
    rank = basis.shape[0]
    pairs = couplings.shape[0]
    group = panels // rank
    partners, rows, half = send_a.shape
    after, before = (n + 1) % narrow, (n + narrow - 1) % narrow
    me_a, me_b = x * narrow + n, w * 2 + core

    def device_a(p):
        return (z * short + p // narrow, p % narrow)

    def device_b(p):
        return (p // 2, y * 2 + p % 2)

    groups = ((me_a, device_a, ((label_a, code_a), (send_a, got_a))), (me_b, device_b, ((label_b, code_b), (send_b, got_b))))

    barrier = pltpu.get_barrier_semaphore()

    @pl.loop(1, partners)
    def _(step):
        for me, device, _ in groups:
            pl.semaphore_signal(barrier, inc=1, device_id=device((me + step) % partners), device_id_type=MESH)

    loads = [
        pltpu.make_async_copy(source, target, local_sem.at[i])
        for i, (source, target) in enumerate(
            ((excitation, own_field), (basis, own_basis), (couplings, own_couplings), (coords, own_coords))
        )
    ]
    for load in loads:
        load.start()

    dest_along = dest[...]
    dest_down = jnp.broadcast_to(dest_along.astype(F32), (128, pairs)).T
    source_down[...] = jnp.broadcast_to(origin[...].astype(F32), (128, pairs)).T
    orders = []
    for p in range(0, pairs, 128):
        same = (dest_down == dest_along[:, p : p + 128].astype(F32)) & (iota((pairs, 128), 0) < iota((pairs, 128), 1) + p)
        orders.append(jnp.sum(jnp.where(same, 1.0, 0.0), axis=0, keepdims=True))
    order = jnp.concatenate(orders, 1).astype(jnp.int32)
    places = placement(sizes, dest_along, order)

    loads[0].wait()
    for c in range(clusters):
        field[clusters + c] = own_field[:, c * panels : (c + 1) * panels]
    for load in loads[1:]:
        load.wait()
    for c in range(clusters):
        coefficients[c * rank : (c + 1) * rank, :] = lax.dot_general(
            own_basis[:, c * panels : (c + 1) * panels], field[clusters + c], NT, preferred_element_type=F32
        ).astype(BF)

    pl.semaphore_wait(barrier, 2 * (partners - 1))

    halo = []
    middle = field.at[pl.ds(clusters, clusters)]
    for i, (source, target, device) in enumerate((
        (middle, field.at[pl.ds(0, clusters)], after),
        (middle, field.at[pl.ds(2 * clusters, clusters)], before),
        (own_coords, coord_before, after),
        (own_coords, coord_after, before),
    )):
        copy = pltpu.make_async_remote_copy(
            src_ref=source, dst_ref=target, send_sem=halo_send.at[i], recv_sem=halo_recv.at[i],
            device_id=(w, device), device_id_type=MESH,
        )
        copy.start()
        halo.append(copy)

    block = 64
    lane = iota((block, 128), 1)
    for q in range(0, pairs, block):
        at = slice(q, q + block)
        mine = [source_down[at, :] == (lane // rank + g * group).astype(F32) for g in range(clusters // group)]
        for pair in range(rank // 2):
            products = []
            for a in (2 * pair, 2 * pair + 1):
                across = own_couplings[at, (a // group) * 128 : (a // group + 1) * 128].astype(F32)
                tiled = jnp.take_along_axis(across, (a % group) * rank + lane % rank, axis=1)
                chosen = jnp.concatenate([jnp.where(m, tiled, 0.0).astype(BF) for m in mine], 1)
                products.append(jnp.dot(chosen, coefficients[...], preferred_element_type=F32))
            records[at, pair * 128 : (pair + 1) * 128] = jnp.concatenate(products, 1).astype(BF)

    for g, ((partner, row, part), (me, device, streams)) in enumerate(zip(places, groups)):
        (label, code), (send, got) = streams
        position = partner * rows + row
        for p in range(0, partners, 16):
            choice = onehot(position == iota((16 * rows, pairs), 0) + p * rows)
            packed = jnp.dot(choice, records[:, g * half : (g + 1) * half], preferred_element_type=F32).astype(BF)
            send[p : p + 16] = packed.reshape(16, rows, half)
        numbers = (slot[...] + clusters * part + 1).astype(F32)
        left = jnp.where(partner == iota((partners, pairs), 0), numbers, 0.0).astype(BF)
        table = lax.dot_general(left, onehot(row == iota((128, pairs), 0)), NT, preferred_element_type=F32)
        for p in range(partners):
            label[p] = table[p : p + 1]

        @pl.loop(1, partners)
        def _(step):
            there = (me + step) % partners
            for i, (source, target) in enumerate(streams):
                pltpu.make_async_remote_copy(
                    src_ref=source.at[there], dst_ref=target.at[me],
                    send_sem=first_send.at[2 * g + i], recv_sem=first_recv.at[2 * g + i],
                    device_id=device(there), device_id_type=MESH,
                ).start()

        for i, (source, target) in enumerate(streams):
            pltpu.make_async_copy(source.at[me], target.at[me], first_recv.at[2 * g + i]).start()

    raw[...] = jnp.zeros_like(raw)
    ones = jnp.ones((3, own), F32)
    lane_group = iota((panels, panels), 1) // 16

    def prepare(i, part):
        where = part[...].astype(F32)
        square = where[0:1] * where[0:1] + where[1:2] * where[1:2] + where[2:3] * where[2:3]
        if i == 1:
            raw[0:3, :] = where
            raw[6:9, :] = ones
            for row, value in enumerate(split(square + SOFTEN)):
                raw[3 + row : 4 + row, :] = value
            rows = raw[...].astype(BF)
            for r in range(group):
                targets[16 * r : 16 * r + 16, :] = rows
        raw[0:3, :] = -2.0 * where
        raw[3:6, :] = ones
        for row, value in enumerate(split(square)):
            raw[6 + row : 7 + row, :] = value
        for g in range(clusters // group):
            block = jnp.concatenate(
                [raw[:, (group * g + r) * panels : (group * g + r + 1) * panels] for r in range(group)], axis=0
            ).T
            for r in range(group):
                sources[i * clusters + group * g + r] = jnp.where(lane_group == r, block, 0.0).astype(BF)

    prepare(1, own_coords)
    for copy in halo:
        copy.wait()
    prepare(0, coord_before)
    prepare(2, coord_after)

    @pl.when(n == 0)
    def _():
        field[0:clusters] = jnp.zeros((clusters, columns, panels), BF)

    @pl.when(n == narrow - 1)
    def _():
        field[2 * clusters : 3 * clusters] = jnp.zeros((clusters, columns, panels), BF)

    scale = 1.0 / math.sqrt(panels * entries)

    def near_clusters(start, stop):
        @pl.loop(start, stop)
        def _(cluster):
            cut = pl.ds(pl.multiple_of(cluster * panels, panels), panels)
            target = targets[:, cut]
            total = jnp.zeros((columns, panels), F32)
            for entry in range(entries):
                source = lists[entry, cluster]
                distance = jnp.dot(sources[source], target, preferred_element_type=F32)
                kernel = lax.rsqrt(distance).astype(BF)
                total += jnp.dot(field[source], kernel, preferred_element_type=F32)
            near[:, cut] = total * scale

    for g, (got, code, part, final) in enumerate(((got_a, code_a, part_a, sum_a), (got_b, code_b, part_b, sum_b))):
        near_clusters(0 if g == 0 else FIRST_NEAR, FIRST_NEAR if g == 0 else SECOND_NEAR)
        pltpu.make_async_copy(code, code, first_recv.at[2 * g]).wait()
        pltpu.make_async_copy(got, got, first_recv.at[2 * g + 1]).wait()
        for p in range(partners):
            codes[p : p + 1, :] = code[p]
        slots = partners * rows
        copied = jnp.dot(
            onehot(iota((slots, partners), 0) // rows == iota((slots, partners), 1)),
            codes[...].astype(BF),
            preferred_element_type=F32,
        )
        picked = jnp.where(iota((slots, 128), 0) % rows == iota((slots, 128), 1), copied, 0.0).astype(BF)
        along = lax.dot_general(jnp.ones((8, 128), BF), picked, NT, preferred_element_type=F32)[0:1].astype(jnp.int32)
        arrived = got[...].reshape(slots, half)
        for p in range(0, last, 2):
            choice = onehot(along == iota((2 * clusters, slots), 0) + (p * clusters + 1))
            sums = jnp.dot(choice, arrived, preferred_element_type=F32).astype(BF)
            part[p : p + 2] = sums.reshape(2, clusters, half)
        me = z if g == 0 else y

        @pl.loop(1, last)
        def _(step):
            there = (me + step) % last
            device = (there * short + x, n) if g == 0 else (w, there * 2 + core)
            pltpu.make_async_remote_copy(
                src_ref=part.at[there], dst_ref=final.at[me], send_sem=last_send.at[g], recv_sem=last_recv.at[g],
                device_id=device, device_id_type=MESH,
            ).start()

        pltpu.make_async_copy(part.at[me], final.at[me], last_recv.at[g]).start()

    near_clusters(SECOND_NEAR, clusters)

    count = rank // 2
    for g, final in enumerate((sum_a, sum_b)):
        pltpu.make_async_copy(final, final, last_recv.at[g]).wait()
        total = final[0].astype(F32)
        for p in range(1, last):
            total += final[p].astype(F32)
        total = total.astype(BF).astype(F32)
        for a in range(count):
            at = (g * count + a) * clusters
            spread[at : at + clusters, :] = total[:, a * columns : (a + 1) * columns]
    for c in range(clusters):
        cut = slice(c * panels, (c + 1) * panels)
        weights = spread[pl.ds(c, rank, stride=clusters), :].T.astype(BF)
        far = jnp.dot(weights, own_basis[:, cut], preferred_element_type=F32)
        out[:, cut] = (near[:, cut] + far).astype(BF)

    for g, (me, device, streams) in enumerate(groups):
        for i, (send, got) in enumerate(streams):
            most = pl.ds(0, partners - 1)
            pltpu.make_async_copy(send.at[most], send.at[most], first_send.at[2 * g + i]).wait()
    for g, part in enumerate((part_a, part_b)):
        most = pl.ds(0, last - 1)
        pltpu.make_async_copy(part.at[most], part.at[most], last_send.at[g]).wait()


def shards(excitation, coords, basis, couplings, near_list, far_dest, far_slot, far_src):
    columns, own = excitation.shape
    clusters, entries = near_list.shape
    panels = own // clusters
    rank = basis.shape[0]
    pairs, squared = couplings.shape
    wide, narrow = lax.axis_size("wide"), lax.axis_size("narrow")
    last = narrow // 2
    partners, rows, half = wide * narrow // last, 2 * last, columns * rank // 2
    dma = pltpu.SemaphoreType.DMA
    return pl.pallas_call(
        functools.partial(main_kernel, (wide, narrow), clusters, entries),
        out_shape=jax.ShapeDtypeStruct((columns, own), BF),
        in_specs=[pl.BlockSpec(memory_space=pltpu.SMEM)] + [ANYWHERE] * 4 + [WHOLE] * 3,
        out_specs=WHOLE,
        scratch_shapes=[
            pltpu.VMEM((3 * clusters, columns, panels), BF),
            pltpu.VMEM(coords.shape, BF),
            pltpu.VMEM(coords.shape, BF),
            pltpu.VMEM((16, own), F32),
            pltpu.VMEM((3 * clusters, panels, panels), BF),
            pltpu.VMEM((panels, own), BF),
            pltpu.VMEM((columns, own), F32),
            pltpu.VMEM(excitation.shape, BF),
            pltpu.VMEM(coords.shape, BF),
            pltpu.VMEM(basis.shape, BF),
            pltpu.VMEM(couplings.shape, BF),
            pltpu.VMEM((pairs, 128), F32),
            pltpu.VMEM((clusters * rank, columns), BF),
            pltpu.VMEM((pairs, 2 * half), BF),
        ]
        + [pltpu.VMEM((partners, rows, half), BF)] * 2
        + [pltpu.VMEM((partners, 1, 128), F32)] * 2
        + [pltpu.VMEM((partners, rows, half), BF)] * 2
        + [pltpu.VMEM((partners, 1, 128), F32)] * 2
        + [pltpu.VMEM((partners, 128), F32)]
        + [pltpu.VMEM((last, clusters, half), BF)] * 4
        + [pltpu.VMEM((rank * clusters, columns), F32)]
        + [dma((4,)), dma((4,)), dma((4,)), dma((4,)), dma((4,)), dma((2,)), dma((2,))],
        compiler_params=pltpu.CompilerParams(vmem_limit_bytes=48 << 20, has_side_effects=True, collective_id=0),
        cost_estimate=pl.CostEstimate(flops=40_000_000_000, bytes_accessed=6_000_000, transcendentals=12_000_000),
    )(
        near_list.T, excitation, coords, basis, couplings,
        far_dest.reshape(1, pairs), far_slot.reshape(1, pairs), far_src.reshape(1, pairs),
    )


def solution(mesh):
    placed = (
        P(None, ("wide", "narrow")),
        P(None, ("wide", "narrow")),
        P(None, ("wide", "narrow")),
        P(("wide", "narrow"), None),
        P(("wide", "narrow"), None),
        P(("wide", "narrow"), None),
        P(("wide", "narrow")),
        P(("wide", "narrow")),
    )
    return jax.shard_map(
        shards, mesh=mesh, in_specs=placed, out_specs=P(None, ("wide", "narrow")), check_vma=False
    )
```

```python
import functools
import math

import jax
import jax.numpy as jnp
from jax import lax
from jax.experimental import pallas as pl
from jax.experimental.pallas import tpu as pltpu
from jax.sharding import PartitionSpec as P

SOFTEN = 0.0025
FIRST_NEAR = 18
SECOND_NEAR = 20
BF = jnp.bfloat16
F32 = jnp.float32
MESH = pl.DeviceIdType.MESH
NT = (((1,), (1,)), ((), ()))
WHOLE = pl.BlockSpec(memory_space=pltpu.VMEM)
ANYWHERE = pl.BlockSpec(memory_space=pltpu.HBM)


def onehot(condition):
    return jnp.where(condition, 1.0, 0.0).astype(BF)


def iota(shape, axis):
    return lax.broadcasted_iota(jnp.int32, shape, axis)


def split(value):
    high = value.astype(BF).astype(F32)
    rest = value - high
    middle = rest.astype(BF).astype(F32)
    return (high, middle, rest - middle)


def placement(sizes, dest, order):
    wide, narrow = sizes
    last = narrow // 2
    first = dest // (narrow * wide // last)
    across = (dest % narrow) // 2
    half_a = (dest % (narrow * wide // last), first * 2 + order, first)
    half_b = ((dest // narrow) * 2 + dest % 2, across * 2 + order, across)
    return (half_a, half_b)


def main_kernel(
    sizes, clusters, entries,
    lists, excitation, coords, basis, couplings, dest, slot, origin,
    out, field, coord_before, coord_after, raw, sources, targets, near,
    own_field, own_coords, own_basis, own_couplings, source_down, coefficients, records,
    send_a, send_b, label_a, label_b,
    got_a, got_b, code_a, code_b, codes, part_a, part_b, sum_a, sum_b, spread,
    local_sem, halo_send, halo_recv, first_send, first_recv, last_send, last_recv, entered,
):
    wide, narrow = sizes
    last = narrow // 2
    short = wide // last
    w, n = lax.axis_index("wide"), lax.axis_index("narrow")
    z, x, y, core = w // short, w % short, n // 2, n % 2
    columns, own = excitation.shape
    panels = own // clusters
    rank = basis.shape[0]
    pairs = couplings.shape[0]
    group = panels // rank
    partners, rows, half = send_a.shape
    after, before = (n + 1) % narrow, (n + narrow - 1) % narrow
    me_a, me_b = x * narrow + n, w * 2 + core

    def device_a(p):
        return (z * short + p // narrow, p % narrow)

    def device_b(p):
        return (p // 2, y * 2 + p % 2)

    groups = ((me_a, device_a, ((label_a, code_a), (send_a, got_a))), (me_b, device_b, ((label_b, code_b), (send_b, got_b))))

    barrier = pltpu.get_barrier_semaphore()

    chip_row = 2 * short
    along_y = [(w, ((y + i) % last) * 2 + core) for i in range(1, last)]
    along_z = [(((z + i) % last) * short + x, n) for i in range(1, last)]

    def say(semaphore, device):
        pl.semaphore_signal(semaphore, inc=1, device_id=device, device_id_type=MESH)

    for i in range(1, chip_row):
        other = (2 * x + core + i) % chip_row
        say(barrier, (z * short + other // 2, 2 * y + other % 2))
    for device in along_y + along_z + [(w, (n + narrow + 2 * core - 1) % narrow)]:
        say(barrier, device)

    loads = [
        pltpu.make_async_copy(source, target, local_sem.at[i])
        for i, (source, target) in enumerate(
            ((excitation, own_field), (basis, own_basis), (couplings, own_couplings), (coords, own_coords))
        )
    ]
    for load in loads:
        load.start()

    dest_along = dest[...]
    dest_down = jnp.broadcast_to(dest_along.astype(F32), (128, pairs)).T
    source_down[...] = jnp.broadcast_to(origin[...].astype(F32), (128, pairs)).T
    orders = []
    for p in range(0, pairs, 128):
        same = (dest_down == dest_along[:, p : p + 128].astype(F32)) & (iota((pairs, 128), 0) < iota((pairs, 128), 1) + p)
        orders.append(jnp.sum(jnp.where(same, 1.0, 0.0), axis=0, keepdims=True))
    order = jnp.concatenate(orders, 1).astype(jnp.int32)
    places = placement(sizes, dest_along, order)

    loads[0].wait()
    for c in range(clusters):
        field[clusters + c] = own_field[:, c * panels : (c + 1) * panels]
    for load in loads[1:]:
        load.wait()
    for c in range(clusters):
        coefficients[c * rank : (c + 1) * rank, :] = lax.dot_general(
            own_basis[:, c * panels : (c + 1) * panels], field[clusters + c], NT, preferred_element_type=F32
        ).astype(BF)

    pl.semaphore_wait(barrier, chip_row - 1 + 2 * (last - 1) + 1)
    for device in along_y + along_z:
        say(entered, device)

    halo = []
    middle = field.at[pl.ds(clusters, clusters)]
    for i, (source, target, device) in enumerate((
        (middle, field.at[pl.ds(0, clusters)], after),
        (middle, field.at[pl.ds(2 * clusters, clusters)], before),
        (own_coords, coord_before, after),
        (own_coords, coord_after, before),
    )):
        copy = pltpu.make_async_remote_copy(
            src_ref=source, dst_ref=target, send_sem=halo_send.at[i], recv_sem=halo_recv.at[i],
            device_id=(w, device), device_id_type=MESH,
        )
        copy.start()
        halo.append(copy)

    block = 64
    lane = iota((block, 128), 1)
    for q in range(0, pairs, block):
        at = slice(q, q + block)
        mine = [source_down[at, :] == (lane // rank + g * group).astype(F32) for g in range(clusters // group)]
        for pair in range(rank // 2):
            products = []
            for a in (2 * pair, 2 * pair + 1):
                across = own_couplings[at, (a // group) * 128 : (a // group + 1) * 128].astype(F32)
                tiled = jnp.take_along_axis(across, (a % group) * rank + lane % rank, axis=1)
                chosen = jnp.concatenate([jnp.where(m, tiled, 0.0).astype(BF) for m in mine], 1)
                products.append(jnp.dot(chosen, coefficients[...], preferred_element_type=F32))
            records[at, pair * 128 : (pair + 1) * 128] = jnp.concatenate(products, 1).astype(BF)

    pl.semaphore_wait(entered, 2 * (last - 1))
    for g, ((partner, row, part), (me, device, streams)) in enumerate(zip(places, groups)):
        (label, code), (send, got) = streams
        position = partner * rows + row
        for p in range(0, partners, 16):
            choice = onehot(position == iota((16 * rows, pairs), 0) + p * rows)
            packed = jnp.dot(choice, records[:, g * half : (g + 1) * half], preferred_element_type=F32).astype(BF)
            send[p : p + 16] = packed.reshape(16, rows, half)
        numbers = (slot[...] + clusters * part + 1).astype(F32)
        left = jnp.where(partner == iota((partners, pairs), 0), numbers, 0.0).astype(BF)
        table = lax.dot_general(left, onehot(row == iota((128, pairs), 0)), NT, preferred_element_type=F32)
        for p in range(partners):
            label[p] = table[p : p + 1]

        @pl.loop(1, partners)
        def _(step):
            there = (me + step) % partners
            for i, (source, target) in enumerate(streams):
                pltpu.make_async_remote_copy(
                    src_ref=source.at[there], dst_ref=target.at[me],
                    send_sem=first_send.at[2 * g + i], recv_sem=first_recv.at[2 * g + i],
                    device_id=device(there), device_id_type=MESH,
                ).start()

        for i, (source, target) in enumerate(streams):
            pltpu.make_async_copy(source.at[me], target.at[me], first_recv.at[2 * g + i]).start()

    raw[...] = jnp.zeros_like(raw)
    ones = jnp.ones((3, own), F32)
    lane_group = iota((panels, panels), 1) // 16

    def prepare(i, part):
        where = part[...].astype(F32)
        square = where[0:1] * where[0:1] + where[1:2] * where[1:2] + where[2:3] * where[2:3]
        if i == 1:
            raw[0:3, :] = where
            raw[6:9, :] = ones
            for row, value in enumerate(split(square + SOFTEN)):
                raw[3 + row : 4 + row, :] = value
            rows = raw[...].astype(BF)
            for r in range(group):
                targets[16 * r : 16 * r + 16, :] = rows
        raw[0:3, :] = -2.0 * where
        raw[3:6, :] = ones
        for row, value in enumerate(split(square)):
            raw[6 + row : 7 + row, :] = value
        for g in range(clusters // group):
            block = jnp.concatenate(
                [raw[:, (group * g + r) * panels : (group * g + r + 1) * panels] for r in range(group)], axis=0
            ).T
            for r in range(group):
                sources[i * clusters + group * g + r] = jnp.where(lane_group == r, block, 0.0).astype(BF)

    prepare(1, own_coords)
    for copy in halo:
        copy.wait()
    prepare(0, coord_before)
    prepare(2, coord_after)

    @pl.when(n == 0)
    def _():
        field[0:clusters] = jnp.zeros((clusters, columns, panels), BF)

    @pl.when(n == narrow - 1)
    def _():
        field[2 * clusters : 3 * clusters] = jnp.zeros((clusters, columns, panels), BF)

    scale = 1.0 / math.sqrt(panels * entries)

    def near_clusters(start, stop):
        @pl.loop(start, stop)
        def _(cluster):
            cut = pl.ds(pl.multiple_of(cluster * panels, panels), panels)
            target = targets[:, cut]
            total = jnp.zeros((columns, panels), F32)
            for entry in range(entries):
                source = lists[entry, cluster]
                distance = jnp.dot(sources[source], target, preferred_element_type=F32)
                kernel = lax.rsqrt(distance).astype(BF)
                total += jnp.dot(field[source], kernel, preferred_element_type=F32)
            near[:, cut] = total * scale

    for g, (got, code, part, final) in enumerate(((got_a, code_a, part_a, sum_a), (got_b, code_b, part_b, sum_b))):
        near_clusters(0 if g == 0 else FIRST_NEAR, FIRST_NEAR if g == 0 else SECOND_NEAR)
        pltpu.make_async_copy(code, code, first_recv.at[2 * g]).wait()
        pltpu.make_async_copy(got, got, first_recv.at[2 * g + 1]).wait()
        for p in range(partners):
            codes[p : p + 1, :] = code[p]
        slots = partners * rows
        copied = jnp.dot(
            onehot(iota((slots, partners), 0) // rows == iota((slots, partners), 1)),
            codes[...].astype(BF),
            preferred_element_type=F32,
        )
        picked = jnp.where(iota((slots, 128), 0) % rows == iota((slots, 128), 1), copied, 0.0).astype(BF)
        along = lax.dot_general(jnp.ones((8, 128), BF), picked, NT, preferred_element_type=F32)[0:1].astype(jnp.int32)
        arrived = got[...].reshape(slots, half)
        for p in range(0, last, 2):
            choice = onehot(along == iota((2 * clusters, slots), 0) + (p * clusters + 1))
            sums = jnp.dot(choice, arrived, preferred_element_type=F32).astype(BF)
            part[p : p + 2] = sums.reshape(2, clusters, half)
        me = z if g == 0 else y

        @pl.loop(1, last)
        def _(step):
            there = (me + step) % last
            device = (there * short + x, n) if g == 0 else (w, there * 2 + core)
            pltpu.make_async_remote_copy(
                src_ref=part.at[there], dst_ref=final.at[me], send_sem=last_send.at[g], recv_sem=last_recv.at[g],
                device_id=device, device_id_type=MESH,
            ).start()

        pltpu.make_async_copy(part.at[me], final.at[me], last_recv.at[g]).start()

    near_clusters(SECOND_NEAR, clusters)

    count = rank // 2
    for g, final in enumerate((sum_a, sum_b)):
        pltpu.make_async_copy(final, final, last_recv.at[g]).wait()
        total = final[0].astype(F32)
        for p in range(1, last):
            total += final[p].astype(F32)
        total = total.astype(BF).astype(F32)
        for a in range(count):
            at = (g * count + a) * clusters
            spread[at : at + clusters, :] = total[:, a * columns : (a + 1) * columns]
    for c in range(clusters):
        cut = slice(c * panels, (c + 1) * panels)
        weights = spread[pl.ds(c, rank, stride=clusters), :].T.astype(BF)
        far = jnp.dot(weights, own_basis[:, cut], preferred_element_type=F32)
        out[:, cut] = (near[:, cut] + far).astype(BF)

    for g, (me, device, streams) in enumerate(groups):
        for i, (send, got) in enumerate(streams):
            most = pl.ds(0, partners - 1)
            pltpu.make_async_copy(send.at[most], send.at[most], first_send.at[2 * g + i]).wait()
    for g, part in enumerate((part_a, part_b)):
        most = pl.ds(0, last - 1)
        pltpu.make_async_copy(part.at[most], part.at[most], last_send.at[g]).wait()


def shards(excitation, coords, basis, couplings, near_list, far_dest, far_slot, far_src):
    columns, own = excitation.shape
    clusters, entries = near_list.shape
    panels = own // clusters
    rank = basis.shape[0]
    pairs, squared = couplings.shape
    wide, narrow = lax.axis_size("wide"), lax.axis_size("narrow")
    last = narrow // 2
    partners, rows, half = wide * narrow // last, 2 * last, columns * rank // 2
    dma = pltpu.SemaphoreType.DMA
    return pl.pallas_call(
        functools.partial(main_kernel, (wide, narrow), clusters, entries),
        out_shape=jax.ShapeDtypeStruct((columns, own), BF),
        in_specs=[pl.BlockSpec(memory_space=pltpu.SMEM)] + [ANYWHERE] * 4 + [WHOLE] * 3,
        out_specs=WHOLE,
        scratch_shapes=[
            pltpu.VMEM((3 * clusters, columns, panels), BF),
            pltpu.VMEM(coords.shape, BF),
            pltpu.VMEM(coords.shape, BF),
            pltpu.VMEM((16, own), F32),
            pltpu.VMEM((3 * clusters, panels, panels), BF),
            pltpu.VMEM((panels, own), BF),
            pltpu.VMEM((columns, own), F32),
            pltpu.VMEM(excitation.shape, BF),
            pltpu.VMEM(coords.shape, BF),
            pltpu.VMEM(basis.shape, BF),
            pltpu.VMEM(couplings.shape, BF),
            pltpu.VMEM((pairs, 128), F32),
            pltpu.VMEM((clusters * rank, columns), BF),
            pltpu.VMEM((pairs, 2 * half), BF),
        ]
        + [pltpu.VMEM((partners, rows, half), BF)] * 2
        + [pltpu.VMEM((partners, 1, 128), F32)] * 2
        + [pltpu.VMEM((partners, rows, half), BF)] * 2
        + [pltpu.VMEM((partners, 1, 128), F32)] * 2
        + [pltpu.VMEM((partners, 128), F32)]
        + [pltpu.VMEM((last, clusters, half), BF)] * 4
        + [pltpu.VMEM((rank * clusters, columns), F32)]
        + [dma((4,)), dma((4,)), dma((4,)), dma((4,)), dma((4,)), dma((2,)), dma((2,))]
        + [pltpu.SemaphoreType.REGULAR],
        compiler_params=pltpu.CompilerParams(vmem_limit_bytes=56 << 20, has_side_effects=True, collective_id=0),
        cost_estimate=pl.CostEstimate(flops=40_000_000_000, bytes_accessed=6_000_000, transcendentals=12_000_000),
    )(
        near_list.T, excitation, coords, basis, couplings,
        far_dest.reshape(1, pairs), far_slot.reshape(1, pairs), far_src.reshape(1, pairs),
    )


def solution(mesh):
    placed = (
        P(None, ("wide", "narrow")),
        P(None, ("wide", "narrow")),
        P(None, ("wide", "narrow")),
        P(("wide", "narrow"), None),
        P(("wide", "narrow"), None),
        P(("wide", "narrow"), None),
        P(("wide", "narrow")),
        P(("wide", "narrow")),
    )
    return jax.shard_map(
        shards, mesh=mesh, in_specs=placed, out_specs=P(None, ("wide", "narrow")), check_vma=False
    )
```

```python
import functools
import math

import jax
import jax.numpy as jnp
from jax import lax
from jax.experimental import pallas as pl
from jax.experimental.pallas import tpu as pltpu
from jax.sharding import PartitionSpec as P

SOFTEN = 0.0025
FIRST_NEAR = 23
SECOND_NEAR = 25
BF = jnp.bfloat16
F32 = jnp.float32
MESH = pl.DeviceIdType.MESH
NT = (((1,), (1,)), ((), ()))
WHOLE = pl.BlockSpec(memory_space=pltpu.VMEM)
ANYWHERE = pl.BlockSpec(memory_space=pltpu.HBM)


def onehot(condition):
    return jnp.where(condition, 1.0, 0.0).astype(BF)


def iota(shape, axis):
    return lax.broadcasted_iota(jnp.int32, shape, axis)


def split(value):
    high = value.astype(BF).astype(F32)
    rest = value - high
    middle = rest.astype(BF).astype(F32)
    return (high, middle, rest - middle)


def placement(sizes, dest, order):
    wide, narrow = sizes
    last = narrow // 2
    first = dest // (narrow * wide // last)
    across = (dest % narrow) // 2
    half_a = (dest % (narrow * wide // last), first * 2 + order, first)
    half_b = ((dest // narrow) * 2 + dest % 2, across * 2 + order, across)
    return (half_a, half_b)


def main_kernel(
    sizes, clusters, entries,
    lists, excitation, coords, basis, couplings, dest, slot, origin,
    out, field, coord_before, coord_after, raw, sources, targets, near,
    own_field, own_coords, own_basis, own_couplings, source_down, coefficients, records,
    send_a, send_b, label_a, label_b,
    got_a, got_b, code_a, code_b, codes, part_a, part_b, sum_a, sum_b, spread,
    local_sem, halo_send, halo_recv, first_send, first_recv, last_send, last_recv, entered,
):
    wide, narrow = sizes
    last = narrow // 2
    short = wide // last
    w, n = lax.axis_index("wide"), lax.axis_index("narrow")
    z, x, y, core = lax.div(w, short), lax.rem(w, short), lax.div(n, 2), lax.rem(n, 2)
    columns, own = excitation.shape
    panels = own // clusters
    rank = basis.shape[0]
    pairs = couplings.shape[0]
    group = panels // rank
    partners, rows, half = send_a.shape
    after, before = lax.rem(n + 1, narrow), lax.rem(n + narrow - 1, narrow)
    me_a, me_b = x * narrow + n, w * 2 + core

    def partners_a(visit):
        for i in range(short):
            column = lax.rem(x + i, short)

            @pl.loop(0 if i else 1, narrow, unroll=3 if i == 0 else 4)
            def _(step):
                there = lax.rem(n + step, narrow)
                visit(column * narrow + there, (z * short + column, there))

    def partners_b(visit):
        for i in range(2):
            side = lax.rem(core + i, 2)

            @pl.loop(0 if i else 1, wide, unroll=4 if i else 1)
            def _(step):
                there = lax.rem(w + step, wide)
                visit(there * 2 + side, (there, y * 2 + side))

    groups = ((me_a, partners_a, ((label_a, code_a), (send_a, got_a))), (me_b, partners_b, ((label_b, code_b), (send_b, got_b))))

    barrier = pltpu.get_barrier_semaphore()

    chip_row = 2 * short
    along_y = [(w, lax.rem(y + i, last) * 2 + core) for i in range(1, last)]
    along_z = [(lax.rem(z + i, last) * short + x, n) for i in range(1, last)]

    def say(semaphore, device):
        pl.semaphore_signal(semaphore, inc=1, device_id=device, device_id_type=MESH)

    for i in range(1, chip_row):
        other = lax.rem(2 * x + core + i, chip_row)
        say(barrier, (z * short + lax.div(other, 2), 2 * y + lax.rem(other, 2)))
    for device in along_y + along_z + [(w, lax.rem(n + narrow + 2 * core - 1, narrow))]:
        say(barrier, device)

    loads = [
        pltpu.make_async_copy(source, target, local_sem.at[i])
        for i, (source, target) in enumerate(
            ((excitation, own_field), (basis, own_basis), (couplings, own_couplings), (coords, own_coords))
        )
    ]
    for load in loads:
        load.start()

    dest_along = dest[...]
    dest_down = jnp.broadcast_to(dest_along.astype(F32), (128, pairs)).T
    source_down[...] = jnp.broadcast_to(origin[...].astype(F32), (128, pairs)).T
    orders = []
    for p in range(0, pairs, 128):
        same = (dest_down == dest_along[:, p : p + 128].astype(F32)) & (iota((pairs, 128), 0) < iota((pairs, 128), 1) + p)
        orders.append(jnp.sum(jnp.where(same, 1.0, 0.0), axis=0, keepdims=True))
    order = jnp.concatenate(orders, 1).astype(jnp.int32)
    places = placement(sizes, dest_along, order)

    loads[0].wait()
    for c in range(clusters):
        field[clusters + c] = own_field[:, c * panels : (c + 1) * panels]
    for load in loads[1:]:
        load.wait()
    for c in range(clusters):
        coefficients[c * rank : (c + 1) * rank, :] = lax.dot_general(
            own_basis[:, c * panels : (c + 1) * panels], field[clusters + c], NT, preferred_element_type=F32
        ).astype(BF)

    pl.semaphore_wait(barrier, chip_row - 1 + 2 * (last - 1) + 1)
    for device in along_y + along_z:
        say(entered, device)

    halo = []
    middle = field.at[pl.ds(clusters, clusters)]
    for i, (source, target, device) in enumerate((
        (middle, field.at[pl.ds(0, clusters)], after),
        (middle, field.at[pl.ds(2 * clusters, clusters)], before),
        (own_coords, coord_before, after),
        (own_coords, coord_after, before),
    )):
        copy = pltpu.make_async_remote_copy(
            src_ref=source, dst_ref=target, send_sem=halo_send.at[i], recv_sem=halo_recv.at[i],
            device_id=(w, device), device_id_type=MESH,
        )
        copy.start()
        halo.append(copy)

    block = 64
    lane = iota((block, 128), 1)
    for g, ((partner, row, part), (me, visits, streams)) in enumerate(zip(places, groups)):
        (label, code), (send, got) = streams
        for q in range(0, pairs, block):
            at = slice(q, q + block)
            mine = [source_down[at, :] == (lane // rank + i * group).astype(F32) for i in range(clusters // group)]
            for pair in range(g * rank // 4, (g + 1) * rank // 4):
                products = []
                for a in (2 * pair, 2 * pair + 1):
                    across = own_couplings[at, (a // group) * 128 : (a // group + 1) * 128].astype(F32)
                    tiled = jnp.take_along_axis(across, (a % group) * rank + lane % rank, axis=1)
                    chosen = jnp.concatenate([jnp.where(m, tiled, 0.0).astype(BF) for m in mine], 1)
                    products.append(jnp.dot(chosen, coefficients[...], preferred_element_type=F32))
                records[at, pair * 128 : (pair + 1) * 128] = jnp.concatenate(products, 1).astype(BF)
        position = partner * rows + row
        for p in range(0, partners, 16):
            choice = onehot(position == iota((16 * rows, pairs), 0) + p * rows)
            packed = jnp.dot(choice, records[:, g * half : (g + 1) * half], preferred_element_type=F32).astype(BF)
            send[p : p + 16] = packed.reshape(16, rows, half)
        numbers = (slot[...] + clusters * part + 1).astype(F32)
        left = jnp.where(partner == iota((partners, pairs), 0), numbers, 0.0).astype(BF)
        table = lax.dot_general(left, onehot(row == iota((128, pairs), 0)), NT, preferred_element_type=F32)
        for p in range(partners):
            label[p] = table[p : p + 1]

        def send_to(there, device):
            for i, (source, target) in enumerate(streams):
                pltpu.make_async_remote_copy(
                    src_ref=source.at[there], dst_ref=target.at[me],
                    send_sem=first_send.at[2 * g + i], recv_sem=first_recv.at[2 * g + i],
                    device_id=device, device_id_type=MESH,
                ).start()

        if g == 0:
            pl.semaphore_wait(entered, 2 * (last - 1))
        visits(send_to)

        for i, (source, target) in enumerate(streams):
            pltpu.make_async_copy(source.at[me], target.at[me], first_recv.at[2 * g + i]).start()

    raw[...] = jnp.zeros_like(raw)
    ones = jnp.ones((3, own), F32)
    lane_group = iota((panels, panels), 1) // 16

    def prepare(i, part):
        where = part[...].astype(F32)
        square = where[0:1] * where[0:1] + where[1:2] * where[1:2] + where[2:3] * where[2:3]
        if i == 1:
            raw[0:3, :] = where
            raw[6:9, :] = ones
            for row, value in enumerate(split(square + SOFTEN)):
                raw[3 + row : 4 + row, :] = value
            rows = raw[...].astype(BF)
            for r in range(group):
                targets[16 * r : 16 * r + 16, :] = rows
        raw[0:3, :] = -2.0 * where
        raw[3:6, :] = ones
        for row, value in enumerate(split(square)):
            raw[6 + row : 7 + row, :] = value
        for g in range(clusters // group):
            block = jnp.concatenate(
                [raw[:, (group * g + r) * panels : (group * g + r + 1) * panels] for r in range(group)], axis=0
            ).T
            for r in range(group):
                sources[i * clusters + group * g + r] = jnp.where(lane_group == r, block, 0.0).astype(BF)

    prepare(1, own_coords)
    for copy in halo:
        copy.wait()
    prepare(0, coord_before)
    prepare(2, coord_after)

    @pl.when(n == 0)
    def _():
        field[0:clusters] = jnp.zeros((clusters, columns, panels), BF)

    @pl.when(n == narrow - 1)
    def _():
        field[2 * clusters : 3 * clusters] = jnp.zeros((clusters, columns, panels), BF)

    scale = 1.0 / math.sqrt(panels * entries)

    def near_clusters(start, stop):
        @pl.loop(start, stop)
        def _(cluster):
            cut = pl.ds(pl.multiple_of(cluster * panels, panels), panels)
            target = targets[:, cut]
            total = jnp.zeros((columns, panels), F32)
            for entry in range(entries):
                source = lists[entry, cluster]
                distance = jnp.dot(sources[source], target, preferred_element_type=F32)
                kernel = lax.rsqrt(distance).astype(BF)
                total += jnp.dot(field[source], kernel, preferred_element_type=F32)
            near[:, cut] = total * scale

    for g, (got, code, part, final) in enumerate(((got_a, code_a, part_a, sum_a), (got_b, code_b, part_b, sum_b))):
        near_clusters(0 if g == 0 else FIRST_NEAR, FIRST_NEAR if g == 0 else SECOND_NEAR)
        pltpu.make_async_copy(code, code, first_recv.at[2 * g]).wait()
        for p in range(partners):
            codes[p : p + 1, :] = code[p]
        slots = partners * rows
        copied = jnp.dot(
            onehot(iota((slots, partners), 0) // rows == iota((slots, partners), 1)),
            codes[...].astype(BF),
            preferred_element_type=F32,
        )
        picked = jnp.where(iota((slots, 128), 0) % rows == iota((slots, 128), 1), copied, 0.0).astype(BF)
        along = lax.dot_general(jnp.ones((8, 128), BF), picked, NT, preferred_element_type=F32)[0:1].astype(jnp.int32)
        pltpu.make_async_copy(got, got, first_recv.at[2 * g + 1]).wait()
        arrived = got[...].reshape(slots, half)
        for p in range(0, last, 2):
            choice = onehot(along == iota((2 * clusters, slots), 0) + (p * clusters + 1))
            sums = jnp.dot(choice, arrived, preferred_element_type=F32).astype(BF)
            part[p : p + 2] = sums.reshape(2, clusters, half)
        me = z if g == 0 else y

        @pl.loop(1, last)
        def _(step):
            there = lax.rem(me + step, last)
            device = (there * short + x, n) if g == 0 else (w, there * 2 + core)
            pltpu.make_async_remote_copy(
                src_ref=part.at[there], dst_ref=final.at[me], send_sem=last_send.at[g], recv_sem=last_recv.at[g],
                device_id=device, device_id_type=MESH,
            ).start()

        pltpu.make_async_copy(part.at[me], final.at[me], last_recv.at[g]).start()

    near_clusters(SECOND_NEAR, clusters)

    count = rank // 2
    for g, final in enumerate((sum_a, sum_b)):
        pltpu.make_async_copy(final, final, last_recv.at[g]).wait()
        total = final[0].astype(F32)
        for p in range(1, last):
            total += final[p].astype(F32)
        total = total.astype(BF).astype(F32)
        for a in range(count):
            at = (g * count + a) * clusters
            spread[at : at + clusters, :] = total[:, a * columns : (a + 1) * columns]
    for c in range(clusters):
        cut = slice(c * panels, (c + 1) * panels)
        weights = spread[pl.ds(c, rank, stride=clusters), :].T.astype(BF)
        far = jnp.dot(weights, own_basis[:, cut], preferred_element_type=F32)
        out[:, cut] = (near[:, cut] + far).astype(BF)

    for g, (me, device, streams) in enumerate(groups):
        for i, (send, got) in enumerate(streams):
            most = pl.ds(0, partners - 1)
            pltpu.make_async_copy(send.at[most], send.at[most], first_send.at[2 * g + i]).wait()
    for g, part in enumerate((part_a, part_b)):
        most = pl.ds(0, last - 1)
        pltpu.make_async_copy(part.at[most], part.at[most], last_send.at[g]).wait()


def shards(excitation, coords, basis, couplings, near_list, far_dest, far_slot, far_src):
    columns, own = excitation.shape
    clusters, entries = near_list.shape
    panels = own // clusters
    rank = basis.shape[0]
    pairs, squared = couplings.shape
    wide, narrow = lax.axis_size("wide"), lax.axis_size("narrow")
    last = narrow // 2
    partners, rows, half = wide * narrow // last, 2 * last, columns * rank // 2
    dma = pltpu.SemaphoreType.DMA
    return pl.pallas_call(
        functools.partial(main_kernel, (wide, narrow), clusters, entries),
        out_shape=jax.ShapeDtypeStruct((columns, own), BF),
        in_specs=[pl.BlockSpec(memory_space=pltpu.SMEM)] + [ANYWHERE] * 4 + [WHOLE] * 3,
        out_specs=WHOLE,
        scratch_shapes=[
            pltpu.VMEM((3 * clusters, columns, panels), BF),
            pltpu.VMEM(coords.shape, BF),
            pltpu.VMEM(coords.shape, BF),
            pltpu.VMEM((16, own), F32),
            pltpu.VMEM((3 * clusters, panels, panels), BF),
            pltpu.VMEM((panels, own), BF),
            pltpu.VMEM((columns, own), F32),
            pltpu.VMEM(excitation.shape, BF),
            pltpu.VMEM(coords.shape, BF),
            pltpu.VMEM(basis.shape, BF),
            pltpu.VMEM(couplings.shape, BF),
            pltpu.VMEM((pairs, 128), F32),
            pltpu.VMEM((clusters * rank, columns), BF),
            pltpu.VMEM((pairs, 2 * half), BF),
        ]
        + [pltpu.VMEM((partners, rows, half), BF)] * 2
        + [pltpu.VMEM((partners, 1, 128), F32)] * 2
        + [pltpu.VMEM((partners, rows, half), BF)] * 2
        + [pltpu.VMEM((partners, 1, 128), F32)] * 2
        + [pltpu.VMEM((partners, 128), F32)]
        + [pltpu.VMEM((last, clusters, half), BF)] * 4
        + [pltpu.VMEM((rank * clusters, columns), F32)]
        + [dma((4,)), dma((4,)), dma((4,)), dma((4,)), dma((4,)), dma((2,)), dma((2,))]
        + [pltpu.SemaphoreType.REGULAR],
        compiler_params=pltpu.CompilerParams(vmem_limit_bytes=56 << 20, has_side_effects=True, collective_id=0),
        cost_estimate=pl.CostEstimate(flops=40_000_000_000, bytes_accessed=6_000_000, transcendentals=12_000_000),
    )(
        near_list.T, excitation, coords, basis, couplings,
        far_dest.reshape(1, pairs), far_slot.reshape(1, pairs), far_src.reshape(1, pairs),
    )


def solution(mesh):
    placed = (
        P(None, ("wide", "narrow")),
        P(None, ("wide", "narrow")),
        P(None, ("wide", "narrow")),
        P(("wide", "narrow"), None),
        P(("wide", "narrow"), None),
        P(("wide", "narrow"), None),
        P(("wide", "narrow")),
        P(("wide", "narrow")),
    )
    return jax.shard_map(
        shards, mesh=mesh, in_specs=placed, out_specs=P(None, ("wide", "narrow")), check_vma=False
    )
```

```python
import functools
import math

import jax
import jax.numpy as jnp
from jax import lax
from jax.experimental import pallas as pl
from jax.experimental.pallas import tpu as pltpu
from jax.sharding import PartitionSpec as P

SOFTEN = 0.0025
FIRST_NEAR = 23
SECOND_NEAR = 25
BF = jnp.bfloat16
F32 = jnp.float32
MESH = pl.DeviceIdType.MESH
NT = (((1,), (1,)), ((), ()))
WHOLE = pl.BlockSpec(memory_space=pltpu.VMEM)
ANYWHERE = pl.BlockSpec(memory_space=pltpu.HBM)


def onehot(condition):
    return jnp.where(condition, 1.0, 0.0).astype(BF)


def iota(shape, axis):
    return lax.broadcasted_iota(jnp.int32, shape, axis)


def split(value):
    high = value.astype(BF).astype(F32)
    rest = value - high
    middle = rest.astype(BF).astype(F32)
    return (high, middle, rest - middle)


def placement(sizes, dest, order):
    wide, narrow = sizes
    last = narrow // 2
    first = dest // (narrow * wide // last)
    across = (dest % narrow) // 2
    half_a = (dest % (narrow * wide // last), first * 2 + order, first)
    half_b = ((dest // narrow) * 2 + dest % 2, across * 2 + order, across)
    return (half_a, half_b)


def main_kernel(
    sizes, clusters, entries,
    lists, excitation, coords, basis, couplings, dest, slot, origin,
    out, field, coord_before, coord_after, raw, sources, targets, near,
    own_field, own_coords, own_basis, own_couplings, source_down, coefficients, records,
    send_a, send_b, label_a, label_b,
    got_a, got_b, code_a, code_b, codes, part_a, part_b, sum_a, sum_b, spread,
    local_sem, halo_send, halo_recv, first_send, first_recv, last_send, last_recv, entered,
):
    wide, narrow = sizes
    last = narrow // 2
    short = wide // last
    w, n = lax.axis_index("wide"), lax.axis_index("narrow")
    z, x, y, core = lax.div(w, short), lax.rem(w, short), lax.div(n, 2), lax.rem(n, 2)
    columns, own = excitation.shape
    panels = own // clusters
    rank = basis.shape[0]
    pairs = couplings.shape[0]
    group = panels // rank
    partners, rows, half = send_a.shape
    after, before = lax.rem(n + 1, narrow), lax.rem(n + narrow - 1, narrow)
    me_a, me_b = x * narrow + n, w * 2 + core

    def both_ways(step, count):
        odd = lax.rem(step, 2)
        return odd * lax.div(step + 1, 2) + (1 - odd) * (count - lax.div(step, 2))

    def partners_a(visit):
        for i in range(short):
            column = lax.rem(x + i, short)

            @pl.loop(0 if i else 1, narrow, unroll=3 if i == 0 else 4)
            def _(step):
                there = lax.rem(n + both_ways(step, narrow), narrow)
                visit(column * narrow + there, (z * short + column, there))

    def partners_b(visit):
        for i in range(2):
            side = lax.rem(core + i, 2)

            @pl.loop(0 if i else 1, wide, unroll=4 if i else 1)
            def _(step):
                there = lax.rem(w + both_ways(step, wide), wide)
                visit(there * 2 + side, (there, y * 2 + side))

    groups = ((me_a, partners_a, ((label_a, code_a), (send_a, got_a))), (me_b, partners_b, ((label_b, code_b), (send_b, got_b))))

    barrier = pltpu.get_barrier_semaphore()

    chip_row = 2 * short
    along_y = [(w, lax.rem(y + i, last) * 2 + core) for i in range(1, last)]
    along_z = [(lax.rem(z + i, last) * short + x, n) for i in range(1, last)]

    def say(semaphore, device):
        pl.semaphore_signal(semaphore, inc=1, device_id=device, device_id_type=MESH)

    for i in range(1, chip_row):
        other = lax.rem(2 * x + core + i, chip_row)
        say(barrier, (z * short + lax.div(other, 2), 2 * y + lax.rem(other, 2)))
    for device in along_y + along_z + [(w, lax.rem(n + narrow + 2 * core - 1, narrow))]:
        say(barrier, device)

    loads = [
        pltpu.make_async_copy(source, target, local_sem.at[i])
        for i, (source, target) in enumerate(
            ((excitation, own_field), (basis, own_basis), (couplings, own_couplings), (coords, own_coords))
        )
    ]
    for load in loads:
        load.start()

    dest_along = dest[...]
    dest_down = jnp.broadcast_to(dest_along.astype(F32), (128, pairs)).T
    source_down[...] = jnp.broadcast_to(origin[...].astype(F32), (128, pairs)).T
    orders = []
    for p in range(0, pairs, 128):
        same = (dest_down == dest_along[:, p : p + 128].astype(F32)) & (iota((pairs, 128), 0) < iota((pairs, 128), 1) + p)
        orders.append(jnp.sum(jnp.where(same, 1.0, 0.0), axis=0, keepdims=True))
    order = jnp.concatenate(orders, 1).astype(jnp.int32)
    places = placement(sizes, dest_along, order)

    loads[0].wait()
    for c in range(clusters):
        field[clusters + c] = own_field[:, c * panels : (c + 1) * panels]
    for load in loads[1:]:
        load.wait()
    for c in range(clusters):
        coefficients[c * rank : (c + 1) * rank, :] = lax.dot_general(
            own_basis[:, c * panels : (c + 1) * panels], field[clusters + c], NT, preferred_element_type=F32
        ).astype(BF)

    pl.semaphore_wait(barrier, chip_row - 1 + 2 * (last - 1) + 1)
    for device in along_y + along_z:
        say(entered, device)

    halo = []
    middle = field.at[pl.ds(clusters, clusters)]
    for i, (source, target, device) in enumerate((
        (middle, field.at[pl.ds(0, clusters)], after),
        (middle, field.at[pl.ds(2 * clusters, clusters)], before),
        (own_coords, coord_before, after),
        (own_coords, coord_after, before),
    )):
        copy = pltpu.make_async_remote_copy(
            src_ref=source, dst_ref=target, send_sem=halo_send.at[i], recv_sem=halo_recv.at[i],
            device_id=(w, device), device_id_type=MESH,
        )
        copy.start()
        halo.append(copy)

    block = 64
    lane = iota((block, 128), 1)
    for g, ((partner, row, part), (me, visits, streams)) in enumerate(zip(places, groups)):
        (label, code), (send, got) = streams
        for q in range(0, pairs, block):
            at = slice(q, q + block)
            mine = [source_down[at, :] == (lane // rank + i * group).astype(F32) for i in range(clusters // group)]
            for pair in range(g * rank // 4, (g + 1) * rank // 4):
                products = []
                for a in (2 * pair, 2 * pair + 1):
                    across = own_couplings[at, (a // group) * 128 : (a // group + 1) * 128].astype(F32)
                    tiled = jnp.take_along_axis(across, (a % group) * rank + lane % rank, axis=1)
                    chosen = jnp.concatenate([jnp.where(m, tiled, 0.0).astype(BF) for m in mine], 1)
                    products.append(jnp.dot(chosen, coefficients[...], preferred_element_type=F32))
                records[at, pair * 128 : (pair + 1) * 128] = jnp.concatenate(products, 1).astype(BF)
        position = partner * rows + row
        for p in range(0, partners, 16):
            choice = onehot(position == iota((16 * rows, pairs), 0) + p * rows)
            packed = jnp.dot(choice, records[:, g * half : (g + 1) * half], preferred_element_type=F32).astype(BF)
            send[p : p + 16] = packed.reshape(16, rows, half)
        numbers = (slot[...] + clusters * part + 1).astype(F32)
        left = jnp.where(partner == iota((partners, pairs), 0), numbers, 0.0).astype(BF)
        table = lax.dot_general(left, onehot(row == iota((128, pairs), 0)), NT, preferred_element_type=F32)
        for p in range(partners):
            label[p] = table[p : p + 1]

        def send_to(there, device):
            for i, (source, target) in enumerate(streams):
                pltpu.make_async_remote_copy(
                    src_ref=source.at[there], dst_ref=target.at[me],
                    send_sem=first_send.at[2 * g + i], recv_sem=first_recv.at[2 * g + i],
                    device_id=device, device_id_type=MESH,
                ).start()

        if g == 0:
            pl.semaphore_wait(entered, 2 * (last - 1))
        visits(send_to)

        for i, (source, target) in enumerate(streams):
            pltpu.make_async_copy(source.at[me], target.at[me], first_recv.at[2 * g + i]).start()

    raw[...] = jnp.zeros_like(raw)
    ones = jnp.ones((3, own), F32)
    lane_group = iota((panels, panels), 1) // 16

    def prepare(i, part):
        where = part[...].astype(F32)
        square = where[0:1] * where[0:1] + where[1:2] * where[1:2] + where[2:3] * where[2:3]
        if i == 1:
            raw[0:3, :] = where
            raw[6:9, :] = ones
            for row, value in enumerate(split(square + SOFTEN)):
                raw[3 + row : 4 + row, :] = value
            rows = raw[...].astype(BF)
            for r in range(group):
                targets[16 * r : 16 * r + 16, :] = rows
        raw[0:3, :] = -2.0 * where
        raw[3:6, :] = ones
        for row, value in enumerate(split(square)):
            raw[6 + row : 7 + row, :] = value
        for g in range(clusters // group):
            block = jnp.concatenate(
                [raw[:, (group * g + r) * panels : (group * g + r + 1) * panels] for r in range(group)], axis=0
            ).T
            for r in range(group):
                sources[i * clusters + group * g + r] = jnp.where(lane_group == r, block, 0.0).astype(BF)

    prepare(1, own_coords)
    for copy in halo:
        copy.wait()
    prepare(0, coord_before)
    prepare(2, coord_after)

    @pl.when(n == 0)
    def _():
        field[0:clusters] = jnp.zeros((clusters, columns, panels), BF)

    @pl.when(n == narrow - 1)
    def _():
        field[2 * clusters : 3 * clusters] = jnp.zeros((clusters, columns, panels), BF)

    scale = 1.0 / math.sqrt(panels * entries)

    def near_clusters(start, stop):
        @pl.loop(start, stop)
        def _(cluster):
            cut = pl.ds(pl.multiple_of(cluster * panels, panels), panels)
            target = targets[:, cut]
            total = jnp.zeros((columns, panels), F32)
            for entry in range(entries):
                source = lists[entry, cluster]
                distance = jnp.dot(sources[source], target, preferred_element_type=F32)
                kernel = lax.rsqrt(distance).astype(BF)
                total += jnp.dot(field[source], kernel, preferred_element_type=F32)
            near[:, cut] = total * scale

    for g, (got, code, part, final) in enumerate(((got_a, code_a, part_a, sum_a), (got_b, code_b, part_b, sum_b))):
        near_clusters(0 if g == 0 else FIRST_NEAR, FIRST_NEAR if g == 0 else SECOND_NEAR)
        pltpu.make_async_copy(code, code, first_recv.at[2 * g]).wait()
        for p in range(partners):
            codes[p : p + 1, :] = code[p]
        slots = partners * rows
        copied = jnp.dot(
            onehot(iota((slots, partners), 0) // rows == iota((slots, partners), 1)),
            codes[...].astype(BF),
            preferred_element_type=F32,
        )
        picked = jnp.where(iota((slots, 128), 0) % rows == iota((slots, 128), 1), copied, 0.0).astype(BF)
        along = lax.dot_general(jnp.ones((8, 128), BF), picked, NT, preferred_element_type=F32)[0:1].astype(jnp.int32)
        pltpu.make_async_copy(got, got, first_recv.at[2 * g + 1]).wait()
        arrived = got[...].reshape(slots, half)
        for p in range(0, last, 2):
            choice = onehot(along == iota((2 * clusters, slots), 0) + (p * clusters + 1))
            sums = jnp.dot(choice, arrived, preferred_element_type=F32).astype(BF)
            part[p : p + 2] = sums.reshape(2, clusters, half)
        me = z if g == 0 else y

        @pl.loop(1, last)
        def _(step):
            there = lax.rem(me + both_ways(step, last), last)
            device = (there * short + x, n) if g == 0 else (w, there * 2 + core)
            pltpu.make_async_remote_copy(
                src_ref=part.at[there], dst_ref=final.at[me], send_sem=last_send.at[g], recv_sem=last_recv.at[g],
                device_id=device, device_id_type=MESH,
            ).start()

        pltpu.make_async_copy(part.at[me], final.at[me], last_recv.at[g]).start()

    near_clusters(SECOND_NEAR, clusters)

    count = rank // 2
    for g, final in enumerate((sum_a, sum_b)):
        pltpu.make_async_copy(final, final, last_recv.at[g]).wait()
        total = final[0].astype(F32)
        for p in range(1, last):
            total += final[p].astype(F32)
        total = total.astype(BF).astype(F32)
        for a in range(count):
            at = (g * count + a) * clusters
            spread[at : at + clusters, :] = total[:, a * columns : (a + 1) * columns]
    for c in range(clusters):
        cut = slice(c * panels, (c + 1) * panels)
        weights = spread[pl.ds(c, rank, stride=clusters), :].T.astype(BF)
        far = jnp.dot(weights, own_basis[:, cut], preferred_element_type=F32)
        out[:, cut] = (near[:, cut] + far).astype(BF)

    for g, (me, device, streams) in enumerate(groups):
        for i, (send, got) in enumerate(streams):
            most = pl.ds(0, partners - 1)
            pltpu.make_async_copy(send.at[most], send.at[most], first_send.at[2 * g + i]).wait()
    for g, part in enumerate((part_a, part_b)):
        most = pl.ds(0, last - 1)
        pltpu.make_async_copy(part.at[most], part.at[most], last_send.at[g]).wait()


def shards(excitation, coords, basis, couplings, near_list, far_dest, far_slot, far_src):
    columns, own = excitation.shape
    clusters, entries = near_list.shape
    panels = own // clusters
    rank = basis.shape[0]
    pairs, squared = couplings.shape
    wide, narrow = lax.axis_size("wide"), lax.axis_size("narrow")
    last = narrow // 2
    partners, rows, half = wide * narrow // last, 2 * last, columns * rank // 2
    dma = pltpu.SemaphoreType.DMA
    return pl.pallas_call(
        functools.partial(main_kernel, (wide, narrow), clusters, entries),
        out_shape=jax.ShapeDtypeStruct((columns, own), BF),
        in_specs=[pl.BlockSpec(memory_space=pltpu.SMEM)] + [ANYWHERE] * 4 + [WHOLE] * 3,
        out_specs=WHOLE,
        scratch_shapes=[
            pltpu.VMEM((3 * clusters, columns, panels), BF),
            pltpu.VMEM(coords.shape, BF),
            pltpu.VMEM(coords.shape, BF),
            pltpu.VMEM((16, own), F32),
            pltpu.VMEM((3 * clusters, panels, panels), BF),
            pltpu.VMEM((panels, own), BF),
            pltpu.VMEM((columns, own), F32),
            pltpu.VMEM(excitation.shape, BF),
            pltpu.VMEM(coords.shape, BF),
            pltpu.VMEM(basis.shape, BF),
            pltpu.VMEM(couplings.shape, BF),
            pltpu.VMEM((pairs, 128), F32),
            pltpu.VMEM((clusters * rank, columns), BF),
            pltpu.VMEM((pairs, 2 * half), BF),
        ]
        + [pltpu.VMEM((partners, rows, half), BF)] * 2
        + [pltpu.VMEM((partners, 1, 128), F32)] * 2
        + [pltpu.VMEM((partners, rows, half), BF)] * 2
        + [pltpu.VMEM((partners, 1, 128), F32)] * 2
        + [pltpu.VMEM((partners, 128), F32)]
        + [pltpu.VMEM((last, clusters, half), BF)] * 4
        + [pltpu.VMEM((rank * clusters, columns), F32)]
        + [dma((4,)), dma((4,)), dma((4,)), dma((4,)), dma((4,)), dma((2,)), dma((2,))]
        + [pltpu.SemaphoreType.REGULAR],
        compiler_params=pltpu.CompilerParams(vmem_limit_bytes=56 << 20, has_side_effects=True, collective_id=0),
        cost_estimate=pl.CostEstimate(flops=40_000_000_000, bytes_accessed=6_000_000, transcendentals=12_000_000),
    )(
        near_list.T, excitation, coords, basis, couplings,
        far_dest.reshape(1, pairs), far_slot.reshape(1, pairs), far_src.reshape(1, pairs),
    )


def solution(mesh):
    placed = (
        P(None, ("wide", "narrow")),
        P(None, ("wide", "narrow")),
        P(None, ("wide", "narrow")),
        P(("wide", "narrow"), None),
        P(("wide", "narrow"), None),
        P(("wide", "narrow"), None),
        P(("wide", "narrow")),
        P(("wide", "narrow")),
    )
    return jax.shard_map(
        shards, mesh=mesh, in_specs=placed, out_specs=P(None, ("wide", "narrow")), check_vma=False
    )
```

```python
import functools
import math

import jax
import jax.numpy as jnp
from jax import lax
from jax.experimental import pallas as pl
from jax.experimental.pallas import tpu as pltpu
from jax.sharding import PartitionSpec as P

SOFTEN = 0.0025
FIRST_NEAR = 22
SECOND_NEAR = 22
BF = jnp.bfloat16
F32 = jnp.float32
MESH = pl.DeviceIdType.MESH
NT = (((1,), (1,)), ((), ()))
WHOLE = pl.BlockSpec(memory_space=pltpu.VMEM)
ANYWHERE = pl.BlockSpec(memory_space=pltpu.HBM)


def onehot(condition):
    return jnp.where(condition, 1.0, 0.0).astype(BF)


def iota(shape, axis):
    return lax.broadcasted_iota(jnp.int32, shape, axis)


def split(value):
    high = value.astype(BF).astype(F32)
    rest = value - high
    middle = rest.astype(BF).astype(F32)
    return (high, middle, rest - middle)


def placement(sizes, dest, order):
    wide, narrow = sizes
    last = narrow // 2
    first = dest // (narrow * wide // last)
    across = (dest % narrow) // 2
    half_a = (dest % (narrow * wide // last), first * 2 + order, first)
    half_b = ((dest // narrow) * 2 + dest % 2, across * 2 + order, across)
    return (half_a, half_b)


def main_kernel(
    sizes, clusters, entries,
    lists, excitation, coords, basis, couplings, dest, slot, origin,
    out, field, coord_before, coord_after, raw, sources, targets, near,
    own_field, own_coords, own_basis, own_couplings, source_down, coefficients, records,
    send_a, send_b, label_a, label_b,
    got_a, got_b, code_a, code_b, codes, part_a, part_b, sum_a, sum_b, spread,
    local_sem, halo_send, halo_recv, first_send, first_recv, last_send, last_recv, entered,
):
    wide, narrow = sizes
    last = narrow // 2
    short = wide // last
    w, n = lax.axis_index("wide"), lax.axis_index("narrow")
    z, x, y, core = lax.div(w, short), lax.rem(w, short), lax.div(n, 2), lax.rem(n, 2)
    columns, own = excitation.shape
    panels = own // clusters
    rank = basis.shape[0]
    pairs = couplings.shape[0]
    group = panels // rank
    partners, rows, half = send_a.shape
    after, before = lax.rem(n + 1, narrow), lax.rem(n + narrow - 1, narrow)
    me_a, me_b = x * narrow + n, w * 2 + core

    def partners_a(visit):
        for i in range(short):
            column = lax.rem(x + i, short)

            @pl.loop(0 if i else 1, narrow, unroll=3 if i == 0 else 4)
            def _(step):
                there = lax.rem(n + step, narrow)
                visit(column * narrow + there, (z * short + column, there))

    def partners_b(visit):
        for i in range(2):
            side = lax.rem(core + i, 2)

            @pl.loop(0 if i else 1, wide, unroll=4 if i else 1)
            def _(step):
                there = lax.rem(w + step, wide)
                visit(there * 2 + side, (there, y * 2 + side))

    groups = ((me_a, partners_a, ((label_a, code_a), (send_a, got_a))), (me_b, partners_b, ((label_b, code_b), (send_b, got_b))))

    barrier = pltpu.get_barrier_semaphore()

    chip_row = 2 * short
    along_y = [(w, lax.rem(y + i, last) * 2 + core) for i in range(1, last)]
    along_z = [(lax.rem(z + i, last) * short + x, n) for i in range(1, last)]

    def say(semaphore, device):
        pl.semaphore_signal(semaphore, inc=1, device_id=device, device_id_type=MESH)

    for i in range(1, chip_row):
        other = lax.rem(2 * x + core + i, chip_row)
        say(barrier, (z * short + lax.div(other, 2), 2 * y + lax.rem(other, 2)))
    for device in along_y + along_z + [(w, lax.rem(n + narrow + 2 * core - 1, narrow))]:
        say(barrier, device)

    loads = [
        pltpu.make_async_copy(source, target, local_sem.at[i])
        for i, (source, target) in enumerate(
            ((excitation, own_field), (basis, own_basis), (couplings, own_couplings), (coords, own_coords))
        )
    ]
    for load in loads:
        load.start()

    dest_along = dest[...]
    dest_down = jnp.broadcast_to(dest_along.astype(F32), (128, pairs)).T
    source_down[...] = jnp.broadcast_to(origin[...].astype(F32), (128, pairs)).T
    orders = []
    for p in range(0, pairs, 128):
        same = (dest_down == dest_along[:, p : p + 128].astype(F32)) & (iota((pairs, 128), 0) < iota((pairs, 128), 1) + p)
        orders.append(jnp.sum(jnp.where(same, 1.0, 0.0), axis=0, keepdims=True))
    order = jnp.concatenate(orders, 1).astype(jnp.int32)
    places = placement(sizes, dest_along, order)

    loads[0].wait()
    for c in range(clusters):
        field[clusters + c] = own_field[:, c * panels : (c + 1) * panels]
    for load in loads[1:]:
        load.wait()
    for c in range(clusters):
        coefficients[c * rank : (c + 1) * rank, :] = lax.dot_general(
            own_basis[:, c * panels : (c + 1) * panels], field[clusters + c], NT, preferred_element_type=F32
        ).astype(BF)

    pl.semaphore_wait(barrier, chip_row - 1 + 2 * (last - 1) + 1)
    for device in along_y + along_z:
        say(entered, device)

    halo = []
    middle = field.at[pl.ds(clusters, clusters)]
    for i, (source, target, device) in enumerate((
        (middle, field.at[pl.ds(0, clusters)], after),
        (middle, field.at[pl.ds(2 * clusters, clusters)], before),
        (own_coords, coord_before, after),
        (own_coords, coord_after, before),
    )):
        copy = pltpu.make_async_remote_copy(
            src_ref=source, dst_ref=target, send_sem=halo_send.at[i], recv_sem=halo_recv.at[i],
            device_id=(w, device), device_id_type=MESH,
        )
        copy.start()
        halo.append(copy)

    block = 64
    lane = iota((block, 128), 1)
    for g, ((partner, row, part), (me, visits, streams)) in enumerate(zip(places, groups)):
        (label, code), (send, got) = streams
        for q in range(0, pairs, block):
            at = slice(q, q + block)
            mine = [source_down[at, :] == (lane // rank + i * group).astype(F32) for i in range(clusters // group)]
            for pair in range(g * rank // 4, (g + 1) * rank // 4):
                products = []
                for a in (2 * pair, 2 * pair + 1):
                    across = own_couplings[at, (a // group) * 128 : (a // group + 1) * 128].astype(F32)
                    tiled = jnp.take_along_axis(across, (a % group) * rank + lane % rank, axis=1)
                    chosen = jnp.concatenate([jnp.where(m, tiled, 0.0).astype(BF) for m in mine], 1)
                    products.append(jnp.dot(chosen, coefficients[...], preferred_element_type=F32))
                records[at, pair * 128 : (pair + 1) * 128] = jnp.concatenate(products, 1).astype(BF)
        position = partner * rows + row
        for p in range(0, partners, 16):
            choice = onehot(position == iota((16 * rows, pairs), 0) + p * rows)
            packed = jnp.dot(choice, records[:, g * half : (g + 1) * half], preferred_element_type=F32).astype(BF)
            send[p : p + 16] = packed.reshape(16, rows, half)
        numbers = (slot[...] + clusters * part + 1).astype(F32)
        left = jnp.where(partner == iota((partners, pairs), 0), numbers, 0.0).astype(BF)
        table = lax.dot_general(left, onehot(row == iota((128, pairs), 0)), NT, preferred_element_type=F32)
        for p in range(partners):
            label[p] = table[p : p + 1]

        def send_to(there, device):
            for i, (source, target) in enumerate(streams):
                pltpu.make_async_remote_copy(
                    src_ref=source.at[there], dst_ref=target.at[me],
                    send_sem=first_send.at[2 * g + i], recv_sem=first_recv.at[2 * g + i],
                    device_id=device, device_id_type=MESH,
                ).start()

        if g == 0:
            pl.semaphore_wait(entered, 2 * (last - 1))
        visits(send_to)

        for i, (source, target) in enumerate(streams):
            pltpu.make_async_copy(source.at[me], target.at[me], first_recv.at[2 * g + i]).start()

    raw[...] = jnp.zeros_like(raw)
    ones = jnp.ones((3, own), F32)
    lane_group = iota((panels, panels), 1) // 16

    def prepare(i, part):
        where = part[...].astype(F32)
        square = where[0:1] * where[0:1] + where[1:2] * where[1:2] + where[2:3] * where[2:3]
        if i == 1:
            raw[0:3, :] = where
            raw[6:9, :] = ones
            for row, value in enumerate(split(square + SOFTEN)):
                raw[3 + row : 4 + row, :] = value
            rows = raw[...].astype(BF)
            for r in range(group):
                targets[16 * r : 16 * r + 16, :] = rows
        raw[0:3, :] = -2.0 * where
        raw[3:6, :] = ones
        for row, value in enumerate(split(square)):
            raw[6 + row : 7 + row, :] = value
        for g in range(clusters // group):
            block = jnp.concatenate(
                [raw[:, (group * g + r) * panels : (group * g + r + 1) * panels] for r in range(group)], axis=0
            ).T
            for r in range(group):
                sources[i * clusters + group * g + r] = jnp.where(lane_group == r, block, 0.0).astype(BF)

    prepare(1, own_coords)
    for copy in halo:
        copy.wait()
    prepare(0, coord_before)
    prepare(2, coord_after)

    @pl.when(n == 0)
    def _():
        field[0:clusters] = jnp.zeros((clusters, columns, panels), BF)

    @pl.when(n == narrow - 1)
    def _():
        field[2 * clusters : 3 * clusters] = jnp.zeros((clusters, columns, panels), BF)

    scale = 1.0 / math.sqrt(panels * entries)

    def near_clusters(start, stop):
        @pl.loop(start, stop)
        def _(cluster):
            cut = pl.ds(pl.multiple_of(cluster * panels, panels), panels)
            target = targets[:, cut]
            total = jnp.zeros((columns, panels), F32)
            for entry in range(entries):
                source = lists[entry, cluster]
                distance = jnp.dot(sources[source], target, preferred_element_type=F32)
                kernel = lax.rsqrt(distance).astype(BF)
                total += jnp.dot(field[source], kernel, preferred_element_type=F32)
            near[:, cut] = total * scale

    for g, (got, code, part, final) in enumerate(((got_a, code_a, part_a, sum_a), (got_b, code_b, part_b, sum_b))):
        near_clusters(0 if g == 0 else FIRST_NEAR, FIRST_NEAR if g == 0 else SECOND_NEAR)
        pltpu.make_async_copy(code, code, first_recv.at[2 * g]).wait()
        for p in range(partners):
            codes[p : p + 1, :] = code[p]
        slots = partners * rows
        copied = jnp.dot(
            onehot(iota((slots, partners), 0) // rows == iota((slots, partners), 1)),
            codes[...].astype(BF),
            preferred_element_type=F32,
        )
        picked = jnp.where(iota((slots, 128), 0) % rows == iota((slots, 128), 1), copied, 0.0).astype(BF)
        along = lax.dot_general(jnp.ones((8, 128), BF), picked, NT, preferred_element_type=F32)[0:1].astype(jnp.int32)
        pltpu.make_async_copy(got, got, first_recv.at[2 * g + 1]).wait()
        arrived = got[...].reshape(slots, half)
        for p in range(0, last, 2):
            choice = onehot(along == iota((2 * clusters, slots), 0) + (p * clusters + 1))
            sums = jnp.dot(choice, arrived, preferred_element_type=F32).astype(BF)
            part[p : p + 2] = sums.reshape(2, clusters, half)
        me = z if g == 0 else y

        @pl.loop(1, last)
        def _(step):
            there = lax.rem(me + step, last)
            device = (there * short + x, n) if g == 0 else (w, there * 2 + core)
            pltpu.make_async_remote_copy(
                src_ref=part.at[there], dst_ref=final.at[me], send_sem=last_send.at[g], recv_sem=last_recv.at[g],
                device_id=device, device_id_type=MESH,
            ).start()

        pltpu.make_async_copy(part.at[me], final.at[me], last_recv.at[g]).start()

    near_clusters(SECOND_NEAR, clusters)

    count = rank // 2
    for g, final in enumerate((sum_a, sum_b)):
        pltpu.make_async_copy(final, final, last_recv.at[g]).wait()
        total = final[0].astype(F32)
        for p in range(1, last):
            total += final[p].astype(F32)
        total = total.astype(BF).astype(F32)
        for a in range(count):
            at = (g * count + a) * clusters
            spread[at : at + clusters, :] = total[:, a * columns : (a + 1) * columns]
    for c in range(clusters):
        cut = slice(c * panels, (c + 1) * panels)
        weights = spread[pl.ds(c, rank, stride=clusters), :].T.astype(BF)
        far = jnp.dot(weights, own_basis[:, cut], preferred_element_type=F32)
        out[:, cut] = (near[:, cut] + far).astype(BF)

    for g, (me, device, streams) in enumerate(groups):
        for i, (send, got) in enumerate(streams):
            most = pl.ds(0, partners - 1)
            pltpu.make_async_copy(send.at[most], send.at[most], first_send.at[2 * g + i]).wait()
    for g, part in enumerate((part_a, part_b)):
        most = pl.ds(0, last - 1)
        pltpu.make_async_copy(part.at[most], part.at[most], last_send.at[g]).wait()


def shards(excitation, coords, basis, couplings, near_list, far_dest, far_slot, far_src):
    columns, own = excitation.shape
    clusters, entries = near_list.shape
    panels = own // clusters
    rank = basis.shape[0]
    pairs, squared = couplings.shape
    wide, narrow = lax.axis_size("wide"), lax.axis_size("narrow")
    last = narrow // 2
    partners, rows, half = wide * narrow // last, 2 * last, columns * rank // 2
    dma = pltpu.SemaphoreType.DMA
    return pl.pallas_call(
        functools.partial(main_kernel, (wide, narrow), clusters, entries),
        out_shape=jax.ShapeDtypeStruct((columns, own), BF),
        in_specs=[pl.BlockSpec(memory_space=pltpu.SMEM)] + [ANYWHERE] * 4 + [WHOLE] * 3,
        out_specs=WHOLE,
        scratch_shapes=[
            pltpu.VMEM((3 * clusters, columns, panels), BF),
            pltpu.VMEM(coords.shape, BF),
            pltpu.VMEM(coords.shape, BF),
            pltpu.VMEM((16, own), F32),
            pltpu.VMEM((3 * clusters, panels, panels), BF),
            pltpu.VMEM((panels, own), BF),
            pltpu.VMEM((columns, own), F32),
            pltpu.VMEM(excitation.shape, BF),
            pltpu.VMEM(coords.shape, BF),
            pltpu.VMEM(basis.shape, BF),
            pltpu.VMEM(couplings.shape, BF),
            pltpu.VMEM((pairs, 128), F32),
            pltpu.VMEM((clusters * rank, columns), BF),
            pltpu.VMEM((pairs, 2 * half), BF),
        ]
        + [pltpu.VMEM((partners, rows, half), BF)] * 2
        + [pltpu.VMEM((partners, 1, 128), F32)] * 2
        + [pltpu.VMEM((partners, rows, half), BF)] * 2
        + [pltpu.VMEM((partners, 1, 128), F32)] * 2
        + [pltpu.VMEM((partners, 128), F32)]
        + [pltpu.VMEM((last, clusters, half), BF)] * 4
        + [pltpu.VMEM((rank * clusters, columns), F32)]
        + [dma((4,)), dma((4,)), dma((4,)), dma((4,)), dma((4,)), dma((2,)), dma((2,))]
        + [pltpu.SemaphoreType.REGULAR],
        compiler_params=pltpu.CompilerParams(vmem_limit_bytes=56 << 20, has_side_effects=True, collective_id=0),
        cost_estimate=pl.CostEstimate(flops=40_000_000_000, bytes_accessed=6_000_000, transcendentals=12_000_000),
    )(
        near_list.T, excitation, coords, basis, couplings,
        far_dest.reshape(1, pairs), far_slot.reshape(1, pairs), far_src.reshape(1, pairs),
    )


def solution(mesh):
    placed = (
        P(None, ("wide", "narrow")),
        P(None, ("wide", "narrow")),
        P(None, ("wide", "narrow")),
        P(("wide", "narrow"), None),
        P(("wide", "narrow"), None),
        P(("wide", "narrow"), None),
        P(("wide", "narrow")),
        P(("wide", "narrow")),
    )
    return jax.shard_map(
        shards, mesh=mesh, in_specs=placed, out_specs=P(None, ("wide", "narrow")), check_vma=False
    )
```
